256 devices in a mesh: dp: 2 (over y_lo), ctx: 16 (over y_hi, z), head: 8 (over x, core).
Axes of the slice: x: 4, y: 4 (y_hi: 2, y_lo: 2; y = y_hi * 2 + y_lo), z: 8, core: 2. Of those that a mesh axis runs over, the one named last changes fastest.
Arguments:
- queries: bfloat16 [2, 4096, 8192], P('dp', 'ctx', 'head'), may hold values from -45 to 45
- keys: bfloat16 [2, 4096, 1024], P('dp', 'ctx', 'head'), may hold values from -6 to 6
- values: bfloat16 [2, 4096, 1024], P('dp', 'ctx', 'head'), may hold values from -6 to 6
- doc_ids: int32 [2, 4096], P('dp'), may hold values from 0 to 2, never falling along the last dimension, each value on 1 to 3072 neighbouring positions
- inputs: bfloat16 [2, 4096, 8192], P('dp', 'ctx', 'head'), may hold values from -6 to 6
- gate_input: bfloat16 [2, 4096, 8192], P('dp', 'ctx', 'head'), may hold values from -40 to 40
- b_input: bfloat16 [2, 4096, 1024], P('dp', 'ctx', 'head'), may hold values from -0.0625 to 0.0625
- c_input: bfloat16 [2, 4096, 1024], P('dp', 'ctx', 'head'), may hold values from -6 to 6
- dt_raw: float32 [2, 4096, 128], P('dp', 'ctx', 'head'), may hold values from -2 to 2
- dt_bias: float32 [128], P('head'), may hold values from -1 to 1
- decay_log: float32 [128], P('head'), may hold values from -12 to -2
- skip: float32 [128], P('head'), may hold values from 0.5 to 2
- gain: float32 [8192], P('head'), may hold values from 0.5 to 1.5
Outputs:
- teacher_out: bfloat16 [2, 4096, 8192], P('dp', 'ctx', 'head')
- student_out: bfloat16 [2, 4096, 8192], P('dp', 'ctx', 'head')
- grad_gain: float32 [8192], P('head')
- grad_skip: float32 [128], P('head')
The draws below stay inside these ranges and needn't reach their ends.
Inputs may be any that keep to these rules, and one draw needn't show every extreme that they name: `doc_ids`: three or fewer documents a sequence, numbered from 0 in order; one of them has 3072 positions.
All inputs are finite; a program needn't handle non-finite values.
Results may differ from the reference program's by a relative error of at most 0.012.
Values may be sent and summed in bfloat16 or wider, within the bound.
A program may use at most 64 MiB of HBM per device.

```python
import math
import jax
import jax.numpy as jnp
import numpy as np
from jax import lax

DH = 128
HQ = 64
KVH = 8
HS = 128
P_SIZE = 64
N = 128
GROUPS = 8
TOK_DEV = 256
STRETCH = 128
LENGTH = 4096
SEQS = 2
DM = 8192


def shared_keys(key):
    shape = (SEQS, LENGTH, KVH * DH)
    return jnp.clip(jax.random.normal(jax.random.fold_in(key, 11), shape, jnp.float32), -6.0, 6.0)


def draw_keys(key, part):
    return shared_keys(key).astype(jnp.bfloat16)


def draw_queries(key, part):
    shape = (SEQS, LENGTH, HQ * DH)
    return jnp.clip(jax.random.normal(jax.random.fold_in(key, 21), shape, jnp.float32), -6.0, 6.0).astype(jnp.bfloat16)


def draw_gate_input(key, part):
    shape = (SEQS, LENGTH, HS * P_SIZE)
    base = jnp.clip(jax.random.normal(jax.random.fold_in(key, 31), shape, jnp.float32), -4.0, 4.0)
    row_scale = jnp.exp(jax.random.uniform(jax.random.fold_in(key, 32), (SEQS, LENGTH, 1), jnp.float32, -1.2, 1.1))
    col_scale = jnp.exp(jax.random.uniform(jax.random.fold_in(key, 33), (1, 1, HS * P_SIZE), jnp.float32, -1.2, 1.1))
    return (base * row_scale * col_scale).astype(jnp.bfloat16)


def draw_dt_raw(key, part):
    blocks = LENGTH // TOK_DEV
    offset = jax.random.uniform(jax.random.fold_in(key, 41), (SEQS, blocks, 1, HS), jnp.float32, -1.0, 1.0)
    noise = jnp.clip(0.3 * jax.random.normal(jax.random.fold_in(key, 42), (SEQS, blocks, TOK_DEV, HS), jnp.float32), -0.9, 0.9)
    return (offset + noise).reshape(SEQS, LENGTH, HS)


def draw_decay_log(key, part):
    share = 0.4
    fast = jax.random.uniform(jax.random.fold_in(key, 51), (HS,), jnp.float32) < share
    quick = jax.random.uniform(jax.random.fold_in(key, 52), (HS,), jnp.float32, jnp.log(1.0 / 30.0), jnp.log(1.0 / 15.0))
    slow = jax.random.uniform(jax.random.fold_in(key, 53), (HS,), jnp.float32, jnp.log(0.3), jnp.log(1.5)) - jnp.log(jnp.float32(LENGTH))
    return jnp.where(fast, quick, slow)


def level_of(stream_key, extent, shards, smallest, largest):
    def one(position, shards_of):
        heights = jax.random.uniform(jax.random.fold_in(jax.random.fold_in(stream_key, 6), position), (shards_of,), jnp.float32, smallest / len(shards), largest / len(shards))
        return jnp.repeat(jnp.exp(heights), extent[position] // shards_of).reshape((-1,) + (1,) * (len(extent) - position - 1))

    loudness = one(*shards[0])
    for cut in shards[1:]:
        loudness = loudness * one(*cut)
    return loudness


def length_profile(amount, total, limit, slope):
    loads = [(1 << 20) // math.isqrt(grade ** slope) + 1 for grade in range(2, amount + 1)]
    rest, holding = total - limit - (amount - 1), [1] * (amount - 1)
    while rest > 0:
        candidates = [i for i in range(amount - 1) if holding[i] < limit]
        mass, budget = sum([loads[i] for i in candidates]), rest
        for i in candidates:
            more = min(limit - holding[i], max(1, budget * loads[i] // mass), rest)
            holding[i] = holding[i] + more
            rest = rest - more
    return np.array([limit] + holding)


def ragged_sizes(own_key, count, total, bound, slope):
    if count == 2:
        one = jax.random.randint(own_key, (), max(1, total - bound), min(bound, total - 1) + 1)
        return jnp.stack([one, total - one])
    sizes = jnp.asarray(length_profile(count, total, bound, slope), jnp.int32)
    pairs = (count - 1) // 2
    donor, sink = sizes[1:1 + 2 * pairs:2], sizes[2:2 + 2 * pairs:2]
    margin = jnp.minimum(donor - 1, bound - sink)
    moved = jax.random.randint(jax.random.fold_in(own_key, 1), (pairs,), 0, 1 << 20) % (margin + 1)
    sizes = sizes.at[1:1 + 2 * pairs:2].set(donor - moved).at[2:2 + 2 * pairs:2].set(sink + moved)
    return sizes[jax.random.permutation(jax.random.fold_in(own_key, 2), count)]


def bell_draw(stream_key, shape, deviation, bound, pieces=(), held_as=jnp.bfloat16):
    loudness = level_of(stream_key, shape, pieces, -0.22, 0.18) if pieces else 1.0
    entries = jax.random.normal(stream_key, shape, jnp.float32) * deviation * loudness
    return jnp.minimum(jnp.maximum(entries, -bound), bound).astype(held_as)


def setup_inputs(seed: int = 0) -> dict:
    splits = jax.random.split(jax.random.key(seed), 14)
    queries = draw_queries(jax.random.fold_in(splits[13], 71), 0)
    keys = draw_keys(jax.random.fold_in(splits[13], 71), 0)
    values = bell_draw(splits[2], (SEQS, LENGTH, KVH * DH), 1.0, 6.0, ((0, 2), (1, 16), (2, 8)))
    doc_ids = jax.vmap(lambda own: jnp.searchsorted(jnp.cumsum(ragged_sizes(own, 3, LENGTH, LENGTH * 3 // 4, 0)), jnp.arange(LENGTH), side="right"))(jax.random.split(splits[3], SEQS)).reshape((SEQS, LENGTH)).astype(jnp.int32)
    inputs = bell_draw(splits[4], (SEQS, LENGTH, HS * P_SIZE), 1.0, 6.0, ((0, 2), (1, 16), (2, 8)))
    gate_input = draw_gate_input(jax.random.fold_in(splits[13], 71), 0)
    b_input = bell_draw(splits[6], (SEQS, LENGTH, GROUPS * N), (N * 64) ** -0.5, 0.0625, ((0, 2), (1, 16), (2, 8)))
    c_input = bell_draw(splits[7], (SEQS, LENGTH, GROUPS * N), 1.0, 6.0, ((0, 2), (1, 16), (2, 8)))
    dt_raw = draw_dt_raw(jax.random.fold_in(splits[13], 71), 0)
    dt_bias = jnp.clip(jax.random.uniform(splits[9], (HS,), jnp.float32, -1.0, 1.0) * level_of(splits[9], (HS,), ((0, 8),), -0.4, 0.0), -1.0, 1.0)
    decay_log = draw_decay_log(jax.random.fold_in(splits[13], 71), 0)
    skip = jnp.clip(0.5 + 1.5 * jax.random.uniform(splits[11], (HS,), jnp.float32) ** level_of(splits[11], (HS,), ((0, 8),), -0.2, 0.2), 0.5, 2.0)
    gain = jnp.clip(1.0 + 0.1 * jax.random.normal(splits[12], (DM,), jnp.float32), 0.5, 1.5)
    return {"queries": queries, "keys": keys, "values": values, "doc_ids": doc_ids, "inputs": inputs, "gate_input": gate_input, "b_input": b_input, "c_input": c_input, "dt_raw": dt_raw, "dt_bias": dt_bias, "decay_log": decay_log, "skip": skip, "gain": gain}


def natural_rows(length, stretch, tok_dev):
    count = length // tok_dev
    place = jnp.arange(length, dtype=jnp.int32)
    block = place // stretch
    front = block < count
    device = jnp.where(front, block, 2 * count - 1 - block)
    offset = jnp.where(front, place % stretch, stretch + place % stretch)
    return (device * tok_dev + offset).astype(jnp.int32)

def stored_positions(length, stretch, tok_dev):
    count = length // tok_dev
    rows = jnp.arange(length, dtype=jnp.int32)
    device = rows // tok_dev
    offset = rows % tok_dev
    block = jnp.where(offset < stretch, device, 2 * count - 1 - device)
    return (block * stretch + offset % stretch).astype(jnp.int32)

def teacher_one(query_rows, key_part, value_part, docs):
    length = query_rows.shape[0]
    per_kv = HQ // KVH
    query_heads = query_rows.reshape(length, HQ, DH).transpose(1, 0, 2)
    key_heads = key_part.reshape(length, KVH, DH).transpose(1, 0, 2)
    value_heads = value_part.reshape(length, KVH, DH).transpose(1, 0, 2)
    place = jnp.arange(length, dtype=jnp.int32)
    allowed = (place[:, None] >= place[None, :]) & (docs[:, None] == docs[None, :])
    scale = 1.0 / jnp.sqrt(jnp.float32(DH))

    def one_head(head):
        query = query_heads[head]
        key = key_heads[head // per_kv]
        value = value_heads[head // per_kv]
        scores = jnp.dot(query, key.T, preferred_element_type=jnp.float32) * scale
        top = lax.optimization_barrier(jnp.max(jnp.where(allowed, scores, -jnp.inf), axis=1, keepdims=True))
        weights = jnp.where(allowed, jnp.exp(scores - top), 0.0)
        total = lax.optimization_barrier(jnp.sum(weights, axis=1, keepdims=True))
        summed = jnp.dot(weights.astype(jnp.bfloat16), value, preferred_element_type=jnp.float32)
        return (summed / total).astype(jnp.bfloat16)
    result = lax.map(one_head, jnp.arange(HQ, dtype=jnp.int32))
    return result.transpose(1, 0, 2).reshape(length, HQ * DH)

def block_terms(xs, bmat, cmat, dt, rate, docs, prior):
    rows, heads, width = xs.shape
    groups, state = (bmat.shape[1], bmat.shape[2])
    per = heads // groups
    cum = jnp.cumsum(rate, axis=0)
    order = jnp.arange(rows, dtype=jnp.int32)
    allowed = (order[:, None] >= order[None, :]) & (docs[:, None] == docs[None, :])
    gram = jnp.einsum('tgn,sgn->gts', cmat.astype(jnp.float32), bmat.astype(jnp.float32))
    spans = cum.T[:, :, None] - cum.T[:, None, :]
    fading = jnp.exp(jnp.where(allowed[None], spans, -jnp.inf))
    mixing = (fading.reshape(groups, per, rows, rows) * gram[:, None] * dt.T.reshape(groups, per, 1, rows)).astype(jnp.bfloat16)
    grouped = xs.reshape(rows, groups, per, width)
    intra = jnp.einsum('gjts,sgjp->tgjp', mixing.astype(jnp.float32), grouped.astype(jnp.float32)).reshape(rows, heads, width)
    final = cum[-1]
    decay = jnp.where(docs[-1] == prior, jnp.exp(final), 0.0)
    tail = jnp.exp(final[None, :] - cum) * dt * (docs == docs[-1]).astype(jnp.float32)[:, None]
    loaded = (tail.reshape(rows, groups, per)[..., None] * bmat[:, :, None, :].astype(jnp.float32)).astype(jnp.bfloat16)
    summary = jnp.einsum('sgjp,sgjn->gjpn', grouped.astype(jnp.float32), loaded.astype(jnp.float32)).reshape(heads, width, state)
    reach = jnp.exp(cum) * (docs == prior).astype(jnp.float32)[:, None]
    return (intra, decay, summary, reach)

def inflow(cmat, state, reach):
    rows, groups, width_n = cmat.shape
    heads = state.shape[0]
    per = heads // groups
    grouped = state.reshape(groups, per, state.shape[1], width_n)
    flow = jnp.einsum('tgn,gjpn->tgjp', cmat.astype(jnp.float32), grouped, precision=lax.Precision.HIGHEST)
    return flow.reshape(rows, heads, state.shape[1]) * reach[:, :, None]

def student_one(xs, bmat, cmat, dt_raw, dt_bias, decay_log, docs):
    length = xs.shape[0]
    count = length // STRETCH
    dt = jax.nn.softplus(dt_raw + dt_bias)
    rate = -dt * jnp.exp(decay_log)
    x_blocks = xs.reshape(count, STRETCH, HS, P_SIZE)
    b_blocks = bmat.reshape(count, STRETCH, GROUPS, N)
    c_blocks = cmat.reshape(count, STRETCH, GROUPS, N)
    dt_blocks = dt.reshape(count, STRETCH, HS)
    rate_blocks = rate.reshape(count, STRETCH, HS)
    doc_blocks = docs.reshape(count, STRETCH)
    priors = jnp.concatenate([jnp.full((1,), -1, jnp.int32), doc_blocks[:-1, -1].astype(jnp.int32)])

    def step(state, items):
        x_b, b_b, c_b, dt_b, rate_b, doc_b, prior_b = items
        intra, decay, summary, reach = block_terms(x_b, b_b, c_b, dt_b, rate_b, doc_b, prior_b)
        inner = intra + inflow(c_b, state, reach)
        state = decay[:, None, None] * state + summary
        return (state, inner)
    start = jnp.zeros((HS, P_SIZE, N), jnp.float32)
    _, mixed = lax.scan(step, start, (x_blocks, b_blocks, c_blocks, dt_blocks, rate_blocks, doc_blocks, priors))
    return mixed.reshape(length, HS, P_SIZE)

def gated_norm(mixed, xs, gate, skip, gain, groups):
    rows, heads, width = mixed.shape
    values_out = mixed + skip[None, :, None] * xs.astype(jnp.float32)
    gated = values_out.reshape(rows, heads * width) * jax.nn.silu(gate.astype(jnp.float32))
    gated = gated.reshape(rows, groups, -1)
    normed = gated * lax.rsqrt(lax.optimization_barrier(jnp.mean(gated * gated, axis=2, keepdims=True)) + 1e-05)
    return normed.reshape(rows, heads * width) * gain

def reference(queries, keys, values, doc_ids, inputs, gate_input, b_input, c_input, dt_raw, dt_bias, decay_log, skip, gain):
    natural = natural_rows(LENGTH, STRETCH, TOK_DEV)
    stored = stored_positions(LENGTH, STRETCH, TOK_DEV)

    def to_natural(array):
        return jnp.take(array, natural, axis=1)
    q_nat, k_nat, v_nat = (to_natural(queries), to_natural(keys), to_natural(values))
    x_nat, g_nat = (to_natural(inputs), to_natural(gate_input))
    b_nat, c_nat, dt_nat = (to_natural(b_input), to_natural(c_input), to_natural(dt_raw))
    teachers = []
    mixes = []
    for seq in range(SEQS):
        teachers.append(teacher_one(q_nat[seq], k_nat[seq], v_nat[seq], doc_ids[seq]))
        mixes.append(student_one(x_nat[seq], b_nat[seq], c_nat[seq], dt_nat[seq], dt_bias, decay_log, doc_ids[seq]))
    teacher_nat = jnp.stack(teachers)
    mixed = jnp.stack(mixes).reshape(SEQS * LENGTH, HS, P_SIZE)
    x_rows = x_nat.reshape(SEQS * LENGTH, HS, P_SIZE)
    g_rows = g_nat.reshape(SEQS * LENGTH, HS * P_SIZE)
    target = teacher_nat.reshape(SEQS * LENGTH, HS * P_SIZE).astype(jnp.float32)

    def loss_fn(gain_p, skip_p):
        normed = gated_norm(mixed, x_rows, g_rows, skip_p, gain_p, GROUPS)
        diff = normed - target
        return (jnp.sum(diff * diff) / (SEQS * LENGTH), normed)
    (grad_gain, grad_skip), normed = jax.grad(loss_fn, argnums=(0, 1), has_aux=True)(gain, skip)
    student_nat = normed.astype(jnp.bfloat16).reshape(SEQS, LENGTH, HS * P_SIZE)
    teacher_out = jnp.take(teacher_nat, stored, axis=1)
    student_out = jnp.take(student_nat, stored, axis=1)
    return (teacher_out, student_out, grad_gain, grad_skip)
```

```python
import functools

import jax
import jax.numpy as jnp
from jax import lax
from jax.experimental import pallas as pl
from jax.experimental.pallas import tpu as pltpu
from jax.sharding import Mesh
from jax.sharding import PartitionSpec as P

DH = 128
BLK = 128
PEERS = [(dy, dz) for dy in range(2) for dz in range(8) if (dy, dz) != (0, 0)]
ALL = [(dd, dy, dz) for dd in range(2) for dy in range(2) for dz in range(8) if (dd, dy, dz) != (0, 0, 0)]
MESH = pl.DeviceIdType.MESH
CTX = ("ctx_0", "ctx_1")
F32 = jnp.float32
BF16 = jnp.bfloat16
HIGH = lax.Precision.HIGHEST
LOW = -1e30
SCORE_SCALE = 1.4426950408889634 / (DH**0.5)


def iota(shape, dim):
    return lax.broadcasted_iota(jnp.int32, shape, dim)


def dot(a, b, **kw):
    return jnp.dot(a, b, preferred_element_type=F32, **kw)


def kernel(
    q_ref, k_ref, v_ref, docs_ref, x_ref, gate_ref, b_ref, c_ref, dtr_ref, small_ref, gain_ref,
    teacher_ref, student_ref, ggain_ref, gskip_ref,
    kv, qt, acc, top, total, doc_start, mixed, reach_wide,
    send_s, recv_s, send_e, recv_e, send_g, recv_g,
    ring_send, ring_recv, yf_send, yf_recv, yb_send, yb_recv,
    s_send, s_recv, e_send, e_recv, g_send, g_recv,
):
    dp = lax.axis_index("dp")
    y = lax.axis_index("ctx_0")
    z = lax.axis_index("ctx_1")
    core = lax.rem(lax.axis_index("head"), 2)
    b = y * 8 + z
    me = dp * 16 + b
    way = 1 - 2 * core

    def zmod(v):
        return lax.rem(v + 16, 8)

    def at(dy, dz):
        return {"ctx_0": lax.rem(y + dy, 2), "ctx_1": zmod(z + dz)}

    barrier = pltpu.get_barrier_semaphore()
    for dd, dy, dz in ALL:
        where = {"dp": lax.rem(dp + dd, 2), **at(dy, dz)}
        pl.semaphore_signal(barrier, inc=1, device_id=where, device_id_type=MESH)

    docs = docs_ref[...]
    n0 = jnp.sum(jnp.sum((docs < 1).astype(F32), axis=0, keepdims=True), axis=1, keepdims=True)
    n1 = jnp.sum(jnp.sum((docs < 2).astype(F32), axis=0, keepdims=True), axis=1, keepdims=True)

    expand = (lax.shift_right_logical(iota((16, 1024), 1), 6) == iota((16, 1024), 0)).astype(F32)

    def wide(v):
        return dot(v, expand, precision=HIGH)

    small = small_ref[...]
    dt_bias, decay_log, skip = small[0:1], small[1:2], small[2:3]
    skip_wide = wide(jnp.broadcast_to(skip, (8, 16)))[0:1]
    row_t = iota((BLK, BLK), 0)
    lane_s = iota((BLK, BLK), 1)
    lower = row_t >= lane_s
    lower_f = lower.astype(F32)
    first_lanes = lane_s < 64

    for half in range(2):
        r0 = half * BLK
        block = b if half == 0 else 31 - b
        first = (block * BLK).astype(F32)
        doc_row = docs_ref[pl.ds(block, 1), :]
        start = jnp.where(doc_row == 0, 0.0, jnp.where(doc_row == 1, n0, n1)) - first
        end = jnp.where(doc_row == 0, n0, jnp.where(doc_row == 1, n1, 4096.0)) - first
        doc_start[half] = jnp.broadcast_to(start + first, (8, BLK))
        start_last = start[:, BLK - 1 : BLK]
        inherited = jnp.sum((start < 0.0).astype(F32), axis=1, keepdims=True)

        raw = dtr_ref[0, r0 : r0 + BLK, :] + dt_bias
        dt = jnp.maximum(raw, 0.0) + jnp.log(1.0 + jnp.exp(-jnp.abs(raw)))
        rate = -dt * jnp.exp(decay_log)
        cum = dot(lower_f, rate, precision=HIGH)
        cum_t = cum.T
        dt_t = dt.T
        last = cum[BLK - 1 : BLK, :]
        rows16 = iota((BLK, 16), 0).astype(F32)
        tail = jnp.where(rows16 >= start_last, jnp.exp(last - cum) * dt, 0.0)
        reach = jnp.where(rows16 < inherited, jnp.exp(cum), 0.0)
        decay = jnp.where(start_last < 0.0, jnp.exp(last), 0.0)
        reach_wide[r0 : r0 + BLK, :] = wide(reach)
        tail_wide = wide(tail)
        decay_wide = wide(jnp.broadcast_to(decay, (8, 16)))[0:1]
        if half == 0:
            decay_front = decay_wide
        else:
            decay_back = decay_wide

        bmat = b_ref[0, r0 : r0 + BLK, :]
        cmat = c_ref[0, r0 : r0 + BLK, :]
        xs = x_ref[0, r0 : r0 + BLK, :]
        loaded = (xs.astype(F32) * tail_wide).astype(BF16)
        state = dot(bmat.T, loaded).astype(BF16)
        for j in range(8):
            for n in range(2):
                send_s[n * 8 + j, half * 64 : half * 64 + 64, :] = state[
                    n * 64 : n * 64 + 64, j * BLK : (j + 1) * BLK
                ]
        gram = lax.dot_general(cmat, bmat, (((1,), (1,)), ((), ())), preferred_element_type=F32)
        gram = jnp.where(lower & (row_t.astype(F32) < end), gram, 0.0)
        for j in range(8):
            cols = slice(j * BLK, (j + 1) * BLK)
            pair = x_ref[0, r0 : r0 + BLK, cols]
            parts = []
            for h in (2 * j, 2 * j + 1):
                fading = jnp.exp(cum[:, h : h + 1] - cum_t[h : h + 1, :])
                parts.append((fading * (gram * dt_t[h : h + 1, :])).astype(BF16))
            zero = jnp.zeros_like(pair)
            stacked = jnp.concatenate(
                [jnp.where(first_lanes, pair, zero), jnp.where(first_lanes, zero, pair)], axis=0
            )
            intra = dot(jnp.concatenate(parts, axis=1), stacked)
            mixed[r0 : r0 + BLK, cols] = intra + skip_wide[:, cols] * pair.astype(F32)

    row16 = iota((16, BLK), 0)
    for j in range(8):
        cols = slice(j * BLK, (j + 1) * BLK)
        rows = jnp.zeros((16, BLK), F32)
        for at_row, values in ((0, decay_front), (2, decay_back)):
            value = values[:, cols]
            high = value.astype(BF16).astype(F32)
            rows = jnp.where(row16 == at_row, high, rows)
            rows = jnp.where(row16 == at_row + 1, value - high, rows)
        for n in range(2):
            send_s[n * 8 + j, 128:144, :] = rows.astype(BF16)

    for half in range(2):
        r0 = half * BLK
        kv[b, half, 0] = k_ref[0, r0 : r0 + BLK, :]
        kv[b, half, 1] = v_ref[0, r0 : r0 + BLK, :]

    pl.semaphore_wait(barrier, len(ALL))

    def source(off):
        return zmod(z + off)

    def ring(off, dist, forward):
        sign = way if forward else -way
        s = y * 8 + source(off)
        lane = 0 if forward else 1
        return pltpu.make_async_remote_copy(
            src_ref=kv.at[s], dst_ref=kv.at[s],
            send_sem=ring_send.at[lane, dist], recv_sem=ring_recv.at[s],
            device_id={"ctx_1": zmod(z + sign)}, device_id_type=MESH,
        )

    def y_front(zs, mine):
        s = (y if mine else 1 - y) * 8 + zs
        return pltpu.make_async_remote_copy(
            src_ref=kv.at[s, 0], dst_ref=kv.at[s, 0], send_sem=yf_send.at[zs], recv_sem=yf_recv.at[zs],
            device_id={"ctx_0": 1 - y}, device_id_type=MESH,
        )

    def y_back(zs, mine):
        s = (y if mine else 1 - y) * 8 + zs
        return pltpu.make_async_remote_copy(
            src_ref=kv.at[s, 1], dst_ref=kv.at[s, 1], send_sem=yb_send.at[zs], recv_sem=yb_recv.at[zs],
            device_id={"ctx_0": 1 - y}, device_id_type=MESH,
        )

    def y_start(zs):
        y_front(zs, True).start()

        @pl.when(y == 1)
        def _():
            y_back(zs, True).start()

    def y_arrived(zs):
        y_front(zs, False).wait_recv()

        @pl.when(y == 0)
        def _():
            y_back(zs, False).wait_recv()

    ring(0, 0, True).start()
    ring(0, 0, False).start()
    y_start(z)

    def s_copy(dy, dz):
        other = at(dy, dz)
        o = other["ctx_0"] * 8 + other["ctx_1"]
        return pltpu.make_async_remote_copy(
            src_ref=send_s.at[o], dst_ref=recv_s.at[b], send_sem=s_send.at[o], recv_sem=s_recv.at[b],
            device_id=other, device_id_type=MESH,
        )

    def e_copy(dy, dz):
        other = at(dy, dz)
        o = other["ctx_0"] * 8 + other["ctx_1"]
        return pltpu.make_async_remote_copy(
            src_ref=send_e.at[o], dst_ref=recv_e.at[b], send_sem=e_send.at[o], recv_sem=e_recv.at[b],
            device_id=other, device_id_type=MESH,
        )

    for dy, dz in PEERS:
        s_copy(dy, dz).start()
    recv_s[b] = send_s[b]

    for half in range(2):
        for h in range(8):
            qt[half, :, h * DH : (h + 1) * DH] = q_ref[
                0, half * BLK : (half + 1) * BLK, h * DH : (h + 1) * DH
            ].T
    top[...] = jnp.full(top.shape, LOW, F32)
    total[...] = jnp.zeros(total.shape, F32)
    acc[...] = jnp.zeros(acc.shape, F32)
    row_f = row_t.astype(F32)

    def item(s, kh, qh, diagonal):
        key = kv[s, kh, 0]
        value_t = kv[s, kh, 1].T
        key_block = jnp.where(kh == 0, s, 31 - s) if not isinstance(kh, int) else (s if kh == 0 else 31 - s)
        start = doc_start[qh][0:1] - (key_block * BLK).astype(F32)
        allowed = row_f >= start
        if diagonal:
            allowed = allowed & (row_t <= lane_s)
        bias = jnp.where(allowed, 0.0, LOW)
        bias = jnp.concatenate([bias, bias], axis=1)
        for c in range(4):
            cols = slice(c * 256, (c + 1) * 256)
            scores = dot(key, qt[qh, :, cols]) * SCORE_SCALE + bias
            old = top[qh, :, cols]
            new = jnp.maximum(old, jnp.max(scores, axis=0, keepdims=True))
            weights = jnp.exp2(scores - new)
            factor = jnp.exp2(old - new)
            total[qh, :, cols] = total[qh, :, cols] * factor + jnp.sum(weights, axis=0, keepdims=True)
            acc[qh, :, cols] = acc[qh, :, cols] * factor + dot(value_t, weights.astype(BF16))
            top[qh, :, cols] = new

    def other_source(s):
        earlier = s < b
        item(s, 0, 1, False)
        pick = jnp.where(earlier, 0, 1)
        item(s, pick, pick, False)

    def sources(ids):
        def step(i, carry):
            s = ids[0]
            for n in range(1, len(ids)):
                s = jnp.where(i == n, ids[n], s)
            other_source(s)
            return carry

        lax.fori_loop(0, len(ids), step, 0)

    item(b, 0, 0, True)
    item(b, 1, 1, True)
    item(b, 0, 1, False)

    def mine(zs):
        return y * 8 + zs

    def theirs(zs):
        return (1 - y) * 8 + zs

    def hop(d):
        ids = []
        up = source(-way * d)
        ring(-way * d, 0, True).wait_recv()
        if d < 4:
            ring(-way * d, d, True).start()
        y_start(up)
        ids.append(mine(up))
        if d < 4:
            down = source(way * d)
            ring(way * d, 0, False).wait_recv()
            if d < 3:
                ring(way * d, d, False).start()
            y_start(down)
            ids.append(mine(down))
        if d == 1:
            y_arrived(z)
            ids.append(theirs(z))
        else:
            for off in (-way * (d - 1), way * (d - 1)):
                y_arrived(source(off))
                ids.append(theirs(source(off)))
        sources(ids)

    hop(1)
    hop(2)

    def s_wait(k):
        @pl.when(k != b)
        def _():
            pltpu.make_async_remote_copy(
                src_ref=send_s.at[k], dst_ref=recv_s.at[k], send_sem=s_send.at[k], recv_sem=s_recv.at[k],
                device_id={"ctx_1": z}, device_id_type=MESH,
            ).wait_recv()

    def forward(k, state):
        s_wait(k)
        send_e[k, 0:64, :] = state.astype(BF16)
        rows = recv_s[k, 128:144, :].astype(F32)
        return (rows[0:1] + rows[1:2]) * state + recv_s[k, 0:64, :].astype(F32)

    def backward(i, state):
        k = 15 - i
        send_e[k, 64:128, :] = state.astype(BF16)
        rows = recv_s[k, 128:144, :].astype(F32)
        return (rows[2:3] + rows[3:4]) * state + recv_s[k, 64:128, :].astype(F32)

    state = lax.fori_loop(0, 16, forward, jnp.zeros((64, BLK), F32))
    lax.fori_loop(0, 16, backward, state)
    for dy, dz in PEERS:
        e_copy(dy, dz).start()
    recv_e[b] = send_e[b]

    hop(3)
    hop(4)
    y_arrived(source(-way * 4))
    other_source(theirs(source(-way * 4)))

    for half in range(2):
        for h in range(8):
            cols = slice(h * DH, (h + 1) * DH)
            out = acc[half, :, cols] / total[half, :, cols]
            teacher_ref[0, half * BLK : (half + 1) * BLK, cols] = out.T.astype(BF16)

    for dy, dz in PEERS:
        other = at(dy, dz)
        o = other["ctx_0"] * 8 + other["ctx_1"]
        pltpu.make_async_remote_copy(
            src_ref=send_e.at[o], dst_ref=recv_e.at[o], send_sem=e_send.at[o], recv_sem=e_recv.at[o],
            device_id=other, device_id_type=MESH,
        ).wait_recv()
    for half in range(2):
        r0 = half * BLK
        cmat = c_ref[0, r0 : r0 + BLK, :]
        for j in range(8):
            cols = slice(j * BLK, (j + 1) * BLK)
            part = slice(half * 64, half * 64 + 64)
            entering = jnp.concatenate([recv_e[j, part, :], recv_e[8 + j, part, :]], axis=0)
            flow = dot(cmat, entering)
            mixed[r0 : r0 + BLK, cols] = mixed[r0 : r0 + BLK, cols] + flow * reach_wide[r0 : r0 + BLK, cols]

    gain = gain_ref[...]
    rows_at_once = 16

    def norm(i, carry):
        by_gain, by_skip = carry
        rows = pl.ds(pl.multiple_of(i * rows_at_once, rows_at_once), rows_at_once)
        gate = gate_ref[0, rows, :].astype(F32)
        silu = gate / (1.0 + jnp.exp(-gate))
        gated = mixed[rows, :] * silu
        mean = jnp.sum(gated * gated, axis=1, keepdims=True) * (1.0 / 1024)
        inv = lax.rsqrt(mean + 1e-05)
        unit = gated * inv
        normed = unit * gain
        student_ref[0, rows, :] = normed.astype(BF16)
        grad = (normed - teacher_ref[0, rows, :].astype(F32)) * (2.0 / 8192)
        g_unit = grad * gain
        along = jnp.sum(g_unit * unit, axis=1, keepdims=True) * (1.0 / 1024)
        g_mixed = (g_unit - unit * along) * inv * silu
        a = grad * unit
        c = g_mixed * x_ref[0, rows, :].astype(F32)
        return by_gain + a[0:8] + a[8:16], by_skip + c[0:8] + c[8:16]

    zero = jnp.zeros((8, 1024), F32)
    by_gain, by_skip = lax.fori_loop(0, 256 // rows_at_once, norm, (zero, zero))
    by_gain = jnp.sum(by_gain, axis=0, keepdims=True)
    by_head = lax.dot_general(
        by_skip, expand, (((1,), (1,)), ((), ())), preferred_element_type=F32, precision=HIGH
    )
    by_head = jnp.sum(by_head, axis=0, keepdims=True)
    for r in range(8):
        send_g[r : r + 1, :] = by_gain[:, r * BLK : (r + 1) * BLK]
    send_g[8:16, :] = jnp.zeros((8, BLK), F32)
    send_g[8:9, 0:16] = by_head

    def g_copy(dd, dy, dz, arriving):
        where = {"dp": lax.rem(dp + dd, 2), **at(dy, dz)}
        o = where["dp"] * 16 + where["ctx_0"] * 8 + where["ctx_1"]
        slot = o if arriving else me
        return pltpu.make_async_remote_copy(
            src_ref=send_g, dst_ref=recv_g.at[slot], send_sem=g_send.at[o], recv_sem=g_recv.at[slot],
            device_id=where, device_id_type=MESH,
        )

    for peer in ALL:
        g_copy(*peer, False).start()
    recv_g[me] = send_g[...]
    for peer in ALL:
        g_copy(*peer, True).wait_recv()
    summed = recv_g[0]
    for n in range(1, 32):
        summed = summed + recv_g[n]
    ggain_ref[...] = summed[0:8]
    gskip_ref[...] = summed[8:9, 0:16]

    for d in range(4):
        ring(0, d, True).wait_send()
    for d in range(3):
        ring(0, d, False).wait_send()
    for zs in range(8):
        y_front(zs, True).wait_send()

        @pl.when(y == 1)
        def _():
            y_back(zs, True).wait_send()

    for dy, dz in PEERS:
        s_copy(dy, dz).wait_send()
        e_copy(dy, dz).wait_send()
    for peer in ALL:
        g_copy(*peer, False).wait_send()


def body(
    queries, keys, values, doc_ids, inputs, gate_input, b_input, c_input, dt_raw, dt_bias, decay_log, skip, gain
):
    small = jnp.stack([dt_bias, decay_log, skip])
    vmem = pl.BlockSpec(memory_space=pltpu.VMEM)
    dma = pltpu.SemaphoreType.DMA
    teacher, student, by_gain, by_skip = pl.pallas_call(
        kernel,
        out_shape=(
            jax.ShapeDtypeStruct((1, 256, 1024), BF16),
            jax.ShapeDtypeStruct((1, 256, 1024), BF16),
            jax.ShapeDtypeStruct((8, 128), F32),
            jax.ShapeDtypeStruct((1, 16), F32),
        ),
        in_specs=[vmem] * 11,
        out_specs=(vmem,) * 4,
        scratch_shapes=[
            pltpu.VMEM((16, 2, 2, BLK, DH), BF16),
            pltpu.VMEM((2, DH, 1024), BF16),
            pltpu.VMEM((2, DH, 1024), F32),
            pltpu.VMEM((2, 1, 1024), F32),
            pltpu.VMEM((2, 1, 1024), F32),
            pltpu.VMEM((2, 8, BLK), F32),
            pltpu.VMEM((256, 1024), F32),
            pltpu.VMEM((256, 1024), F32),
            pltpu.VMEM((16, 144, BLK), BF16),
            pltpu.VMEM((16, 144, BLK), BF16),
            pltpu.VMEM((16, BLK, BLK), BF16),
            pltpu.VMEM((16, BLK, BLK), BF16),
            pltpu.VMEM((16, BLK), F32),
            pltpu.VMEM((32, 16, BLK), F32),
            dma((2, 4)), dma((16,)), dma((8,)), dma((8,)), dma((8,)), dma((8,)),
            dma((16,)), dma((16,)), dma((16,)), dma((16,)), dma((32,)), dma((32,)),
        ],
        compiler_params=pltpu.CompilerParams(
            collective_id=0, has_side_effects=True, vmem_limit_bytes=48 * 1024 * 1024
        ),
    )(
        queries, keys, values, doc_ids.reshape(32, 128), inputs, gate_input, b_input, c_input, dt_raw,
        small, gain.reshape(1, 1024),
    )
    return teacher, student, by_gain.reshape(1024), by_skip.reshape(16)


def solution(mesh):
    split = Mesh(
        mesh.devices.reshape(mesh.shape["dp"], 2, 8, mesh.shape["head"]),
        ("dp", "ctx_0", "ctx_1", "head"),
    )
    rows = P("dp", CTX, "head")
    return jax.shard_map(
        body,
        mesh=split,
        in_specs=(rows, rows, rows, P("dp", None), rows, rows, rows, rows, rows)
        + (P("head"),) * 4,
        out_specs=(rows, rows, P("head"), P("head")),
        check_vma=False,
    )
```

```python
import functools

import jax
import jax.numpy as jnp
from jax import lax
from jax.experimental import pallas as pl
from jax.experimental.pallas import tpu as pltpu
from jax.sharding import Mesh
from jax.sharding import PartitionSpec as P

DH = 128
BLK = 128
PEERS = [(dy, dz) for dy in range(2) for dz in range(8) if (dy, dz) != (0, 0)]
ALL = [(dd, dy, dz) for dd in range(2) for dy in range(2) for dz in range(8) if (dd, dy, dz) != (0, 0, 0)]
MESH = pl.DeviceIdType.MESH
CTX = ("ctx_0", "ctx_1")
F32 = jnp.float32
BF16 = jnp.bfloat16
HIGH = lax.Precision.HIGHEST
LOW = -1e30
SCORE_SCALE = 1.4426950408889634 / (DH**0.5)


def iota(shape, dim):
    return lax.broadcasted_iota(jnp.int32, shape, dim)


def dot(a, b, **kw):
    return jnp.dot(a, b, preferred_element_type=F32, **kw)


def kernel(
    q_hbm, k_hbm, v_hbm, docs_hbm, x_hbm, gate_hbm, b_hbm, c_hbm, dtr_hbm, bias_hbm, decay_hbm, skip_hbm, gain_hbm,
    teacher_hbm, student_hbm, ggain_ref, gskip_ref,
    teacher_ref, student_ref, q_ref, docs_ref, x_ref, gate_ref, b_ref, c_ref, dtr_ref, bias_ref, decay_ref, skip_ref, gain_ref,
    kv, qt, acc, top, total, doc_start, mixed, reach_wide,
    send_s, recv_s, send_d, recv_d, send_e, recv_e, send_g, recv_g,
    in_sem, out_sem, kv_sem, ring_send, ring_recv, y_send, y_recv,
    s_send, s_recv, d_send, d_recv, e_send, e_recv, g_send, g_recv,
):
    dp = lax.axis_index("dp")
    y = lax.axis_index("ctx_0")
    z = lax.axis_index("ctx_1")
    core = lax.rem(lax.axis_index("head"), 2)
    b = y * 8 + z
    me = dp * 16 + b
    way = 1 - 2 * core

    def zmod(v):
        return lax.rem(v + 16, 8)

    def at(dy, dz):
        return {"ctx_0": lax.rem(y + dy, 2), "ctx_1": zmod(z + dz)}

    barrier = pltpu.get_barrier_semaphore()
    for dd, dy, dz in ALL:
        where = {"dp": lax.rem(dp + dd, 2), **at(dy, dz)}
        pl.semaphore_signal(barrier, inc=1, device_id=where, device_id_type=MESH)

    arrays = (
        (docs_hbm, docs_ref), (dtr_hbm, dtr_ref), (bias_hbm, bias_ref), (decay_hbm, decay_ref),
        (skip_hbm, skip_ref), (x_hbm, x_ref), (b_hbm, b_ref), (c_hbm, c_ref),
        (q_hbm, q_ref), (gate_hbm, gate_ref), (gain_hbm, gain_ref),
    )
    loads = [pltpu.make_async_copy(src, dst, in_sem.at[n]) for n, (src, dst) in enumerate(arrays)]
    for load in loads[:8]:
        load.start()
    kv_loads = []
    for half in range(2):
        for n, src in enumerate((k_hbm, v_hbm)):
            kv_loads.append(
                pltpu.make_async_copy(
                    src.at[0, half * BLK : (half + 1) * BLK, :], kv.at[b, half, n], kv_sem.at[half, n]
                )
            )
    for load in kv_loads:
        load.start()
    for load in loads[8:]:
        load.start()
    for load in loads[:8]:
        load.wait()

    docs = docs_ref[...]
    n0 = jnp.sum(jnp.sum((docs < 1).astype(F32), axis=0, keepdims=True), axis=1, keepdims=True)
    n1 = jnp.sum(jnp.sum((docs < 2).astype(F32), axis=0, keepdims=True), axis=1, keepdims=True)

    expand = (lax.shift_right_logical(iota((16, 1024), 1), 6) == iota((16, 1024), 0)).astype(F32)

    def wide(v):
        return dot(v, expand, precision=HIGH)

    skip_wide = wide(jnp.broadcast_to(skip_ref[...], (8, 16)))[0:1]
    row_t = iota((BLK, BLK), 0)
    lane_s = iota((BLK, BLK), 1)
    row_f = row_t.astype(F32)
    lower = row_t >= lane_s
    lower_f = lower.astype(F32)
    first_lanes = lane_s < 64

    def local_terms(half):
        r0 = half * BLK
        block = b if half == 0 else 31 - b
        first = (block * BLK).astype(F32)
        doc_row = docs_ref[pl.ds(block, 1), :]
        start = jnp.where(doc_row == 0, 0.0, jnp.where(doc_row == 1, n0, n1)) - first
        end = jnp.where(doc_row == 0, n0, jnp.where(doc_row == 1, n1, 4096.0)) - first
        doc_start[half] = jnp.broadcast_to(start + first, (8, BLK))
        start_last = start[:, BLK - 1 : BLK]
        inherited = jnp.sum((start < 0.0).astype(F32), axis=1, keepdims=True)

        raw = dtr_ref[0, :, r0 : r0 + BLK].T + bias_ref[...]
        dt = jnp.maximum(raw, 0.0) + jnp.log(1.0 + jnp.exp(-jnp.abs(raw)))
        rate = -dt * jnp.exp(decay_ref[...])
        cum = dot(lower_f, rate, precision=HIGH)
        cum_t = cum.T
        dt_t = dt.T
        last = cum[BLK - 1 : BLK, :]
        rows16 = iota((BLK, 16), 0).astype(F32)
        tail = jnp.where(rows16 >= start_last, jnp.exp(last - cum) * dt, 0.0)
        reach = jnp.where(rows16 < inherited, jnp.exp(cum), 0.0)
        decay = jnp.where(start_last < 0.0, jnp.exp(last), 0.0)
        tail_wide = wide(tail)
        decay_wide = wide(jnp.broadcast_to(decay, (8, 16)))[0:1]

        bmat = b_ref[0, r0 : r0 + BLK, :]
        cmat = c_ref[0, r0 : r0 + BLK, :]
        loaded = (x_ref[0, r0 : r0 + BLK, :].astype(F32) * tail_wide).astype(BF16)
        state = dot(bmat.T, loaded).astype(BF16)
        for j in range(8):
            cols = slice(j * BLK, (j + 1) * BLK)
            send_d[j, half : half + 1, :] = decay_wide[:, cols]
            for n in range(2):
                send_s[n * 8 + j, half] = state[n * 64 : n * 64 + 64, cols]

        def rest():
            reach_wide[r0 : r0 + BLK, :] = wide(reach)
            gram = lax.dot_general(cmat, bmat, (((1,), (1,)), ((), ())), preferred_element_type=F32)
            gram = jnp.where(lower & (row_f < end), gram, 0.0)
            for j in range(8):
                cols = slice(j * BLK, (j + 1) * BLK)
                pair = x_ref[0, r0 : r0 + BLK, cols]
                parts = []
                for h in (2 * j, 2 * j + 1):
                    fading = jnp.exp(cum[:, h : h + 1] - cum_t[h : h + 1, :])
                    parts.append((fading * (gram * dt_t[h : h + 1, :])).astype(BF16))
                zero = jnp.zeros_like(pair)
                stacked = jnp.concatenate(
                    [jnp.where(first_lanes, pair, zero), jnp.where(first_lanes, zero, pair)], axis=0
                )
                intra = dot(jnp.concatenate(parts, axis=1), stacked)
                mixed[r0 : r0 + BLK, cols] = intra + skip_wide[:, cols] * pair.astype(F32)

        return rest

    def source(off):
        return zmod(z + off)

    def ring(off, dist, forward, half):
        s = y * 8 + source(off)
        lane = 0 if forward else 1
        return pltpu.make_async_remote_copy(
            src_ref=kv.at[s, half], dst_ref=kv.at[s, half],
            send_sem=ring_send.at[lane, dist, half], recv_sem=ring_recv.at[s, half],
            device_id={"ctx_1": zmod(z + (way if forward else -way))}, device_id_type=MESH,
        )

    def y_copy(zs, half, mine):
        s = (y if mine else 1 - y) * 8 + zs
        return pltpu.make_async_remote_copy(
            src_ref=kv.at[s, half], dst_ref=kv.at[s, half],
            send_sem=y_send.at[zs, half], recv_sem=y_recv.at[zs, half],
            device_id={"ctx_0": 1 - y}, device_id_type=MESH,
        )

    def y_start(zs, half):
        if half == 0:
            y_copy(zs, 0, True).start()
        else:

            @pl.when(y == 1)
            def _():
                y_copy(zs, 1, True).start()

    def y_arrived(zs):
        y_copy(zs, 0, False).wait_recv()

        @pl.when(y == 0)
        def _():
            y_copy(zs, 1, False).wait_recv()

    def owner(dy, dz):
        other = at(dy, dz)
        return other, other["ctx_0"] * 8 + other["ctx_1"]

    def s_copy(dy, dz, half):
        other, o = owner(dy, dz)
        return pltpu.make_async_remote_copy(
            src_ref=send_s.at[o, half], dst_ref=recv_s.at[b, half],
            send_sem=s_send.at[o, half], recv_sem=s_recv.at[b, half],
            device_id=other, device_id_type=MESH,
        )

    def d_copy(dy, dz):
        other, o = owner(dy, dz)
        return pltpu.make_async_remote_copy(
            src_ref=send_d.at[other["ctx_1"]], dst_ref=recv_d.at[b], send_sem=d_send.at[o], recv_sem=d_recv.at[b],
            device_id=other, device_id_type=MESH,
        )

    def e_copy(dy, dz, half, arriving=False):
        other, o = owner(dy, dz)
        slot = o if arriving else b
        return pltpu.make_async_remote_copy(
            src_ref=send_e.at[o, half], dst_ref=recv_e.at[slot, half],
            send_sem=e_send.at[o, half], recv_sem=e_recv.at[slot, half],
            device_id=other, device_id_type=MESH,
        )

    rest = local_terms(0)
    for load in kv_loads:
        load.wait()
    pl.semaphore_wait(barrier, len(ALL))

    for half in range(2):
        ring(0, 0, True, half).start()
        ring(0, 0, False, half).start()
        y_start(z, half)
    for dy, dz in PEERS:
        s_copy(dy, dz, 0).start()
    rest()
    rest = local_terms(1)
    recv_s[b] = send_s[b]
    recv_d[b] = send_d[z]

    loads[8].wait()
    for half in range(2):
        for h in range(8):
            qt[half, :, h * DH : (h + 1) * DH] = q_ref[
                0, half * BLK : (half + 1) * BLK, h * DH : (h + 1) * DH
            ].T
    top[...] = jnp.full(top.shape, LOW, F32)
    total[...] = jnp.zeros(total.shape, F32)
    acc[...] = jnp.zeros(acc.shape, F32)

    def item(s, kh, qh, diagonal):
        key = kv[s, kh, 0]
        value_t = kv[s, kh, 1].T
        key_block = jnp.where(kh == 0, s, 31 - s) if not isinstance(kh, int) else (s if kh == 0 else 31 - s)
        start = doc_start[qh][0:1] - (key_block * BLK).astype(F32)
        allowed = row_f >= start
        if diagonal:
            allowed = allowed & (row_t <= lane_s)
        bias = jnp.where(allowed, 0.0, LOW)
        bias = jnp.concatenate([bias, bias], axis=1)
        for c in range(4):
            cols = slice(c * 256, (c + 1) * 256)
            scores = dot(key, qt[qh, :, cols]) * SCORE_SCALE + bias
            old = top[qh, :, cols]
            new = jnp.maximum(old, jnp.max(scores, axis=0, keepdims=True))
            weights = jnp.exp2(scores - new)
            factor = jnp.exp2(old - new)
            total[qh, :, cols] = total[qh, :, cols] * factor + jnp.sum(weights, axis=0, keepdims=True)
            acc[qh, :, cols] = acc[qh, :, cols] * factor + dot(value_t, weights.astype(BF16))
            top[qh, :, cols] = new

    def other_source(s):
        item(s, 0, 1, False)
        pick = jnp.where(s < b, 0, 1)
        item(s, pick, pick, False)

    def sources(ids):
        def step(i, carry):
            s = ids[0]
            for n in range(1, len(ids)):
                s = jnp.where(i == n, ids[n], s)
            other_source(s)
            return carry

        lax.fori_loop(0, len(ids), step, 0)

    def mine(zs):
        return y * 8 + zs

    def theirs(zs):
        return (1 - y) * 8 + zs

    def hop(d):
        up = source(-way * d)
        down = source(way * d)
        for half in range(2):
            ring(-way * d, 0, True, half).wait_recv()
            if d < 4:
                ring(-way * d, d, True, half).start()
            y_start(up, half)
            if d < 4:
                ring(way * d, 0, False, half).wait_recv()
                if d < 3:
                    ring(way * d, d, False, half).start()
                y_start(down, half)

    def attend(d):
        ids = [mine(source(-way * d))]
        if d < 4:
            ids.append(mine(source(way * d)))
        if d == 1:
            y_arrived(z)
            ids.append(theirs(z))
        else:
            for off in (-way * (d - 1), way * (d - 1)):
                y_arrived(source(off))
                ids.append(theirs(source(off)))
        sources(ids)

    hop(1)
    for dy, dz in PEERS:
        d_copy(dy, dz).start()
        s_copy(dy, dz, 1).start()
    rest()
    item(b, 0, 0, True)
    item(b, 1, 1, True)
    item(b, 0, 1, False)
    attend(1)
    hop(2)

    def s_wait(k, half):
        @pl.when(k != b)
        def _():
            pltpu.make_async_remote_copy(
                src_ref=send_s.at[k, half], dst_ref=recv_s.at[k, half],
                send_sem=s_send.at[k, half], recv_sem=s_recv.at[k, half],
                device_id={"ctx_1": z}, device_id_type=MESH,
            ).wait_recv()
            if half == 0:
                pltpu.make_async_remote_copy(
                    src_ref=send_d.at[0], dst_ref=recv_d.at[k], send_sem=d_send.at[k], recv_sem=d_recv.at[k],
                    device_id={"ctx_1": z}, device_id_type=MESH,
                ).wait_recv()

    def scan(half, state):
        def step(i, state):
            k = i if half == 0 else 15 - i
            s_wait(k, half)
            send_e[k, half] = state.astype(BF16)
            return recv_d[k, half : half + 1, :] * state + recv_s[k, half].astype(F32)

        state = lax.fori_loop(0, 16, step, state)
        for dy, dz in PEERS:
            e_copy(dy, dz, half).start()
        recv_e[b, half] = send_e[b, half]
        return state

    state = scan(0, jnp.zeros((64, BLK), F32))
    attend(2)
    hop(3)
    scan(1, state)
    attend(3)
    hop(4)
    attend(4)
    y_arrived(source(-way * 4))
    other_source(theirs(source(-way * 4)))

    for load in loads[9:]:
        load.wait()
    gain = gain_ref[...]
    rows_at_once = 16

    def norm(i, carry):
        by_gain, by_skip = carry
        rows = pl.ds(pl.multiple_of(i * rows_at_once, rows_at_once), rows_at_once)
        gate = gate_ref[0, rows, :].astype(F32)
        silu = gate / (1.0 + jnp.exp(-gate))
        gated = mixed[rows, :] * silu
        mean = jnp.sum(gated * gated, axis=1, keepdims=True) * (1.0 / 1024)
        inv = lax.rsqrt(mean + 1e-05)
        unit = gated * inv
        normed = unit * gain
        student_ref[0, rows, :] = normed.astype(BF16)
        grad = (normed - teacher_ref[0, rows, :].astype(F32)) * (2.0 / 8192)
        g_unit = grad * gain
        along = jnp.sum(g_unit * unit, axis=1, keepdims=True) * (1.0 / 1024)
        g_mixed = (g_unit - unit * along) * inv * silu
        a = grad * unit
        c = g_mixed * x_ref[0, rows, :].astype(F32)
        return by_gain + a[0:8] + a[8:16], by_skip + c[0:8] + c[8:16]

    zero = jnp.zeros((8, 1024), F32)
    grads = (zero, zero)
    for half in range(2):
        r0 = half * BLK
        for h in range(8):
            cols = slice(h * DH, (h + 1) * DH)
            out = acc[half, :, cols] / total[half, :, cols]
            teacher_ref[0, r0 : r0 + BLK, cols] = out.T.astype(BF16)
    outputs = (
        pltpu.make_async_copy(teacher_ref, teacher_hbm, out_sem.at[0]),
        pltpu.make_async_copy(student_ref, student_hbm, out_sem.at[1]),
    )
    outputs[0].start()
    for half in range(2):
        r0 = half * BLK
        for dy, dz in PEERS:
            e_copy(dy, dz, half, True).wait_recv()
        cmat = c_ref[0, r0 : r0 + BLK, :]
        for j in range(8):
            cols = slice(j * BLK, (j + 1) * BLK)
            flow = dot(cmat, jnp.concatenate([recv_e[j, half], recv_e[8 + j, half]], axis=0))
            mixed[r0 : r0 + BLK, cols] = mixed[r0 : r0 + BLK, cols] + flow * reach_wide[r0 : r0 + BLK, cols]
        steps = BLK // rows_at_once
        grads = lax.fori_loop(half * steps, (half + 1) * steps, norm, grads)
    by_gain = jnp.sum(grads[0], axis=0, keepdims=True)
    by_head = lax.dot_general(
        grads[1], expand, (((1,), (1,)), ((), ())), preferred_element_type=F32, precision=HIGH
    )
    by_head = jnp.sum(by_head, axis=0, keepdims=True)
    for r in range(8):
        send_g[r : r + 1, :] = by_gain[:, r * BLK : (r + 1) * BLK]
    send_g[8:9, :] = jnp.zeros((1, BLK), F32)
    send_g[8:9, 0:16] = by_head

    def g_copy(dd, dy, dz, arriving):
        where = {"dp": lax.rem(dp + dd, 2), **at(dy, dz)}
        o = where["dp"] * 16 + where["ctx_0"] * 8 + where["ctx_1"]
        slot = o if arriving else me
        return pltpu.make_async_remote_copy(
            src_ref=send_g, dst_ref=recv_g.at[slot], send_sem=g_send.at[o], recv_sem=g_recv.at[slot],
            device_id=where, device_id_type=MESH,
        )

    for peer in ALL:
        g_copy(*peer, False).start()
    outputs[1].start()
    recv_g[me] = send_g[...]
    for peer in ALL:
        g_copy(*peer, True).wait_recv()
    summed = recv_g[0]
    for n in range(1, 32):
        summed = summed + recv_g[n]
    ggain_ref[...] = summed[0:8]
    gskip_ref[...] = summed[8:9, 0:16]

    for output in outputs:
        output.wait()
    for half in range(2):
        for d in range(4):
            ring(0, d, True, half).wait_send()
        for d in range(3):
            ring(0, d, False, half).wait_send()
    for zs in range(8):
        y_copy(zs, 0, True).wait_send()

        @pl.when(y == 1)
        def _():
            y_copy(zs, 1, True).wait_send()

    for dy, dz in PEERS:
        d_copy(dy, dz).wait_send()
        for half in range(2):
            s_copy(dy, dz, half).wait_send()
            e_copy(dy, dz, half).wait_send()
    for peer in ALL:
        g_copy(*peer, False).wait_send()


def hand_on(*refs):
    sources, results, held, (in_sem, out_sem) = refs[0:4], refs[4:8], refs[8:12], refs[12:]
    loads = [pltpu.make_async_copy(a, v, in_sem.at[n]) for n, (a, v) in enumerate(zip(sources, held))]
    stores = [pltpu.make_async_copy(v, a, out_sem.at[n]) for n, (v, a) in enumerate(zip(held, results))]
    for load in loads:
        load.start()
    for load, store in zip(loads, stores):
        load.wait()
        store.start()
    for store in stores:
        store.wait()


def body(
    queries, keys, values, doc_ids, inputs, gate_input, b_input, c_input, dt_raw, dt_bias, decay_log, skip, gain
):
    vmem = pl.BlockSpec(memory_space=pltpu.VMEM)
    dma = pltpu.SemaphoreType.DMA
    teacher, student, by_gain, by_skip = pl.pallas_call(
        kernel,
        out_shape=(
            jax.ShapeDtypeStruct((1, 256, 1024), BF16),
            jax.ShapeDtypeStruct((1, 256, 1024), BF16),
            jax.ShapeDtypeStruct((8, 128), F32),
            jax.ShapeDtypeStruct((1, 16), F32),
        ),
        in_specs=[pl.BlockSpec(memory_space=pl.ANY)] * 13,
        out_specs=(pl.BlockSpec(memory_space=pl.ANY),) * 2 + (vmem,) * 2,
        scratch_shapes=[
            pltpu.VMEM((1, 256, 1024), BF16),
            pltpu.VMEM((1, 256, 1024), BF16),
            pltpu.VMEM((1, 256, 1024), BF16),
            pltpu.VMEM((32, 128), jnp.int32),
            pltpu.VMEM((1, 256, 1024), BF16),
            pltpu.VMEM((1, 256, 1024), BF16),
            pltpu.VMEM((1, 256, 128), BF16),
            pltpu.VMEM((1, 256, 128), BF16),
            pltpu.VMEM((1, 16, 256), F32),
            pltpu.VMEM((1, 16), F32),
            pltpu.VMEM((1, 16), F32),
            pltpu.VMEM((1, 16), F32),
            pltpu.VMEM((1, 1024), F32),
            pltpu.VMEM((16, 2, 2, BLK, DH), BF16),
            pltpu.VMEM((2, DH, 1024), BF16),
            pltpu.VMEM((2, DH, 1024), F32),
            pltpu.VMEM((2, 1, 1024), F32),
            pltpu.VMEM((2, 1, 1024), F32),
            pltpu.VMEM((2, 8, BLK), F32),
            pltpu.VMEM((256, 1024), F32),
            pltpu.VMEM((256, 1024), F32),
            pltpu.VMEM((16, 2, 64, BLK), BF16),
            pltpu.VMEM((16, 2, 64, BLK), BF16),
            pltpu.VMEM((8, 2, BLK), F32),
            pltpu.VMEM((16, 2, BLK), F32),
            pltpu.VMEM((16, 2, 64, BLK), BF16),
            pltpu.VMEM((16, 2, 64, BLK), BF16),
            pltpu.VMEM((9, BLK), F32),
            pltpu.VMEM((32, 9, BLK), F32),
            dma((11,)), dma((2,)), dma((2, 2)), dma((2, 4, 2)), dma((16, 2)), dma((8, 2)), dma((8, 2)),
            dma((16, 2)), dma((16, 2)), dma((16,)), dma((16,)), dma((16, 2)), dma((16, 2)), dma((32,)), dma((32,)),
        ],
        compiler_params=pltpu.CompilerParams(
            collective_id=0, has_side_effects=True, vmem_limit_bytes=67043328
        ),
    )(
        queries, keys, values, doc_ids.reshape(32, 128), inputs, gate_input, b_input, c_input,
        dt_raw.transpose(0, 2, 1), dt_bias.reshape(1, 16), decay_log.reshape(1, 16), skip.reshape(1, 16),
        gain.reshape(1, 1024),
    )
    anywhere = pl.BlockSpec(memory_space=pl.ANY)
    results = (teacher, student, by_gain, by_skip)
    teacher, student, by_gain, by_skip = pl.pallas_call(
        hand_on,
        out_shape=tuple(jax.ShapeDtypeStruct(a.shape, a.dtype) for a in results),
        in_specs=[anywhere] * 4,
        out_specs=(anywhere,) * 4,
        scratch_shapes=[pltpu.VMEM(a.shape, a.dtype) for a in results] + [dma((4,)), dma((4,))],
        compiler_params=pltpu.CompilerParams(vmem_limit_bytes=67043328),
    )(*results)
    return teacher, student, by_gain.reshape(1024), by_skip.reshape(16)


def solution(mesh):
    split = Mesh(
        mesh.devices.reshape(mesh.shape["dp"], 2, 8, mesh.shape["head"]),
        ("dp", "ctx_0", "ctx_1", "head"),
    )
    rows = P("dp", CTX, "head")
    return jax.shard_map(
        body,
        mesh=split,
        in_specs=(rows, rows, rows, P("dp", None), rows, rows, rows, rows, rows)
        + (P("head"),) * 4,
        out_specs=(rows, rows, P("head"), P("head")),
        check_vma=False,
    )
```

```python
import functools

import jax
import jax.numpy as jnp
from jax import lax
from jax.experimental import pallas as pl
from jax.experimental.pallas import tpu as pltpu
from jax.sharding import Mesh
from jax.sharding import PartitionSpec as P

DH = 128
BLK = 128


def distance(dd, dy, dz):
    return min(dz, 8 - dz) + (1 if dd else 2 * dy)


PEERS = sorted(
    [(dy, dz) for dy in range(2) for dz in range(8) if (dy, dz) != (0, 0)], key=lambda p: -distance(0, *p)
)
ALL = sorted(
    [(dd, dy, dz) for dd in range(2) for dy in range(2) for dz in range(8) if (dd, dy, dz) != (0, 0, 0)],
    key=lambda p: -distance(*p),
)
MESH = pl.DeviceIdType.MESH
CTX = ("ctx_0", "ctx_1")
F32 = jnp.float32
BF16 = jnp.bfloat16
HIGH = lax.Precision.HIGHEST
LOW = -1e30
SCORE_SCALE = 1.4426950408889634 / (DH**0.5)


def iota(shape, dim):
    return lax.broadcasted_iota(jnp.int32, shape, dim)


def dot(a, b, **kw):
    return jnp.dot(a, b, preferred_element_type=F32, **kw)


def kernel(
    q_hbm, k_hbm, v_hbm, docs_hbm, x_hbm, gate_hbm, b_hbm, c_hbm, dtr_hbm, bias_hbm, decay_hbm, skip_hbm, gain_hbm,
    teacher_hbm, student_hbm, ggain_ref, gskip_ref,
    teacher_ref, student_ref, q_ref, docs_ref, x_ref, gate_ref, b_ref, c_ref, dtr_ref, bias_ref, decay_ref, skip_ref, gain_ref,
    silu_ref, kv, qt, acc, top, total, doc_start, mixed, reach_wide,
    send_s, recv_s, send_d, recv_d, send_e, recv_e, send_g, recv_g,
    in_sem, out_sem, kv_sem, ring_send, ring_recv, y_send, y_recv,
    s_send, s_recv, d_send, d_recv, e_send, e_recv, g_send, g_recv, ready,
):
    dp = lax.axis_index("dp")
    y = lax.axis_index("ctx_0")
    z = lax.axis_index("ctx_1")
    core = lax.rem(lax.axis_index("head"), 2)
    b = y * 8 + z
    me = dp * 16 + b
    way = 1 - 2 * core

    def zmod(v):
        return lax.rem(v + 16, 8)

    def at(dy, dz):
        return {"ctx_0": lax.rem(y + dy, 2), "ctx_1": zmod(z + dz)}

    barrier = pltpu.get_barrier_semaphore()
    for dy, dz in PEERS:
        pl.semaphore_signal(barrier, inc=1, device_id=at(dy, dz), device_id_type=MESH)
    partner = {"dp": 1 - dp}
    pl.semaphore_signal(barrier, inc=1, device_id=partner, device_id_type=MESH)

    arrays = (
        (docs_hbm, docs_ref), (dtr_hbm, dtr_ref), (bias_hbm, bias_ref), (decay_hbm, decay_ref),
        (skip_hbm, skip_ref), (x_hbm, x_ref), (b_hbm, b_ref), (c_hbm, c_ref),
        (q_hbm, q_ref), (gate_hbm, gate_ref), (gain_hbm, gain_ref),
    )
    loads = [pltpu.make_async_copy(src, dst, in_sem.at[n]) for n, (src, dst) in enumerate(arrays)]
    for load in loads[:8]:
        load.start()
    kv_loads = []
    for half in range(2):
        for n, src in enumerate((k_hbm, v_hbm)):
            kv_loads.append(
                pltpu.make_async_copy(
                    src.at[0, half * BLK : (half + 1) * BLK, :], kv.at[b, half, n], kv_sem.at[half, n]
                )
            )
    for load in kv_loads:
        load.start()
    for load in loads[8:]:
        load.start()
    for load in loads[:8]:
        load.wait()

    docs = docs_ref[...]
    n0 = jnp.sum(jnp.sum((docs < 1).astype(F32), axis=0, keepdims=True), axis=1, keepdims=True)
    n1 = jnp.sum(jnp.sum((docs < 2).astype(F32), axis=0, keepdims=True), axis=1, keepdims=True)

    expand = (lax.shift_right_logical(iota((16, 1024), 1), 6) == iota((16, 1024), 0)).astype(F32)

    def wide(v):
        return dot(v, expand, precision=HIGH)

    skip_wide = wide(jnp.broadcast_to(skip_ref[...], (8, 16)))[0:1]
    row_t = iota((BLK, BLK), 0)
    lane_s = iota((BLK, BLK), 1)
    row_f = row_t.astype(F32)
    lower = row_t >= lane_s
    lower_f = lower.astype(F32)
    first_lanes = lane_s < 64

    def local_terms(half):
        r0 = half * BLK
        block = b if half == 0 else 31 - b
        first = (block * BLK).astype(F32)
        doc_row = docs_ref[pl.ds(block, 1), :]
        start = jnp.where(doc_row == 0, 0.0, jnp.where(doc_row == 1, n0, n1)) - first
        end = jnp.where(doc_row == 0, n0, jnp.where(doc_row == 1, n1, 4096.0)) - first
        doc_start[half] = jnp.broadcast_to(start + first, (8, BLK))
        start_last = start[:, BLK - 1 : BLK]
        inherited = jnp.sum((start < 0.0).astype(F32), axis=1, keepdims=True)

        raw = dtr_ref[0, :, r0 : r0 + BLK].T + bias_ref[...]
        dt = jnp.maximum(raw, 0.0) + jnp.log(1.0 + jnp.exp(-jnp.abs(raw)))
        rate = -dt * jnp.exp(decay_ref[...])
        cum = dot(lower_f, rate, precision=HIGH)
        cum_t = cum.T
        dt_t = dt.T
        last = cum[BLK - 1 : BLK, :]
        rows16 = iota((BLK, 16), 0).astype(F32)
        tail = jnp.where(rows16 >= start_last, jnp.exp(last - cum) * dt, 0.0)
        reach = jnp.where(rows16 < inherited, jnp.exp(cum), 0.0)
        decay = jnp.where(start_last < 0.0, jnp.exp(last), 0.0)
        tail_wide = wide(tail)
        decay_wide = wide(jnp.broadcast_to(decay, (8, 16)))[0:1]

        bmat = b_ref[0, r0 : r0 + BLK, :]
        cmat = c_ref[0, r0 : r0 + BLK, :]
        loaded = (x_ref[0, r0 : r0 + BLK, :].astype(F32) * tail_wide).astype(BF16)
        state = dot(bmat.T, loaded).astype(BF16)
        for j in range(8):
            cols = slice(j * BLK, (j + 1) * BLK)
            send_d[j, half : half + 1, :] = decay_wide[:, cols]
            for n in range(2):
                send_s[n * 8 + j, half] = state[n * 64 : n * 64 + 64, cols]

        def rest():
            reach_wide[r0 : r0 + BLK, :] = wide(reach)
            gram = lax.dot_general(cmat, bmat, (((1,), (1,)), ((), ())), preferred_element_type=F32)
            gram = jnp.where(lower & (row_f < end), gram, 0.0)
            for j in range(8):
                cols = slice(j * BLK, (j + 1) * BLK)
                pair = x_ref[0, r0 : r0 + BLK, cols]
                parts = []
                for h in (2 * j, 2 * j + 1):
                    fading = jnp.exp(cum[:, h : h + 1] - cum_t[h : h + 1, :])
                    parts.append((fading * (gram * dt_t[h : h + 1, :])).astype(BF16))
                zero = jnp.zeros_like(pair)
                stacked = jnp.concatenate(
                    [jnp.where(first_lanes, pair, zero), jnp.where(first_lanes, zero, pair)], axis=0
                )
                intra = dot(jnp.concatenate(parts, axis=1), stacked)
                mixed[r0 : r0 + BLK, cols] = intra + skip_wide[:, cols] * pair.astype(F32)

        return rest

    def source(off):
        return zmod(z + off)

    def ring(off, dist, forward, half):
        s = y * 8 + source(off)
        lane = 0 if forward else 1
        return pltpu.make_async_remote_copy(
            src_ref=kv.at[s, half], dst_ref=kv.at[s, half],
            send_sem=ring_send.at[lane, dist, half], recv_sem=ring_recv.at[s, half],
            device_id={"ctx_1": zmod(z + (way if forward else -way))}, device_id_type=MESH,
        )

    def y_copy(zs, half, mine):
        s = (y if mine else 1 - y) * 8 + zs
        return pltpu.make_async_remote_copy(
            src_ref=kv.at[s, half], dst_ref=kv.at[s, half],
            send_sem=y_send.at[zs, half], recv_sem=y_recv.at[zs, half],
            device_id={"ctx_0": 1 - y}, device_id_type=MESH,
        )

    def y_start(zs, half):
        if half == 0:
            y_copy(zs, 0, True).start()
        else:

            @pl.when(y == 1)
            def _():
                y_copy(zs, 1, True).start()

    def y_arrived(zs):
        y_copy(zs, 0, False).wait_recv()

        @pl.when(y == 0)
        def _():
            y_copy(zs, 1, False).wait_recv()

    def owner(dy, dz):
        other = at(dy, dz)
        return other, other["ctx_0"] * 8 + other["ctx_1"]

    def s_copy(dy, dz, half):
        other, o = owner(dy, dz)
        return pltpu.make_async_remote_copy(
            src_ref=send_s.at[o, half], dst_ref=recv_s.at[b, half],
            send_sem=s_send.at[o, half], recv_sem=s_recv.at[b, half],
            device_id=other, device_id_type=MESH,
        )

    def d_copy(dy, dz):
        other, o = owner(dy, dz)
        return pltpu.make_async_remote_copy(
            src_ref=send_d.at[other["ctx_1"]], dst_ref=recv_d.at[b], send_sem=d_send.at[o], recv_sem=d_recv.at[b],
            device_id=other, device_id_type=MESH,
        )

    def e_copy(dy, dz, half, arriving=False):
        other, o = owner(dy, dz)
        slot = o if arriving else b
        return pltpu.make_async_remote_copy(
            src_ref=send_e.at[o, half], dst_ref=recv_e.at[slot, half],
            send_sem=e_send.at[o, half], recv_sem=e_recv.at[slot, half],
            device_id=other, device_id_type=MESH,
        )

    rests = [local_terms(half) for half in range(2)]
    for load in kv_loads:
        load.wait()
    pl.semaphore_wait(barrier, len(PEERS) + 1)
    pl.semaphore_signal(ready, inc=1, device_id=partner, device_id_type=MESH)
    for half in range(2):
        ring(0, 0, True, half).start()
        ring(0, 0, False, half).start()
        y_start(z, half)
    for dy, dz in PEERS[:8]:
        d_copy(dy, dz).start()
        s_copy(dy, dz, 0).start()
    recv_s[b] = send_s[b]
    recv_d[b] = send_d[z]
    for rest in rests:
        rest()

    loads[8].wait()
    for half in range(2):
        for h in range(8):
            qt[half, :, h * DH : (h + 1) * DH] = q_ref[
                0, half * BLK : (half + 1) * BLK, h * DH : (h + 1) * DH
            ].T
    top[...] = jnp.full(top.shape, LOW, F32)
    total[...] = jnp.zeros(total.shape, F32)
    acc[...] = jnp.zeros(acc.shape, F32)

    def item(s, kh, qh, diagonal):
        key = kv[s, kh, 0]
        value_t = kv[s, kh, 1].T
        key_block = jnp.where(kh == 0, s, 31 - s) if not isinstance(kh, int) else (s if kh == 0 else 31 - s)
        start = doc_start[qh][0:1] - (key_block * BLK).astype(F32)
        allowed = row_f >= start
        if diagonal:
            allowed = allowed & (row_t <= lane_s)
        bias = jnp.where(allowed, 0.0, LOW)
        bias = jnp.concatenate([bias, bias], axis=1)
        for c in range(4):
            cols = slice(c * 256, (c + 1) * 256)
            scores = dot(key, qt[qh, :, cols]) * SCORE_SCALE + bias
            old = top[qh, :, cols]
            new = jnp.maximum(old, jnp.max(scores, axis=0, keepdims=True))
            weights = jnp.exp2(scores - new)
            factor = jnp.exp2(old - new)
            total[qh, :, cols] = total[qh, :, cols] * factor + jnp.sum(weights, axis=0, keepdims=True)
            acc[qh, :, cols] = acc[qh, :, cols] * factor + dot(value_t, weights.astype(BF16))
            top[qh, :, cols] = new

    def other_source(s):
        item(s, 0, 1, False)
        pick = jnp.where(s < b, 0, 1)
        item(s, pick, pick, False)

    def sources(ids):
        def step(i, carry):
            s = ids[0]
            for n in range(1, len(ids)):
                s = jnp.where(i == n, ids[n], s)
            other_source(s)
            return carry

        lax.fori_loop(0, len(ids), step, 0)

    def mine(zs):
        return y * 8 + zs

    def theirs(zs):
        return (1 - y) * 8 + zs

    def hop(d):
        up = source(-way * d)
        down = source(way * d)
        for half in range(2):
            ring(-way * d, 0, True, half).wait_recv()
            if d < 4:
                ring(-way * d, d, True, half).start()
            y_start(up, half)
            if d < 4:
                ring(way * d, 0, False, half).wait_recv()
                if d < 3:
                    ring(way * d, d, False, half).start()
                y_start(down, half)

    def attend(d):
        ids = [mine(source(-way * d))]
        if d < 4:
            ids.append(mine(source(way * d)))
        if d == 1:
            y_arrived(z)
            ids.append(theirs(z))
        else:
            for off in (-way * (d - 1), way * (d - 1)):
                y_arrived(source(off))
                ids.append(theirs(source(off)))
        sources(ids)

    item(b, 0, 0, True)
    item(b, 1, 1, True)
    item(b, 0, 1, False)

    hop(1)
    for dy, dz in PEERS[8:]:
        d_copy(dy, dz).start()
        s_copy(dy, dz, 0).start()
    hop(2)
    for dy, dz in PEERS:
        s_copy(dy, dz, 1).start()
    attend(1)
    hop(3)
    attend(2)

    def s_wait(k, half):
        @pl.when(k != b)
        def _():
            pltpu.make_async_remote_copy(
                src_ref=send_s.at[k, half], dst_ref=recv_s.at[k, half],
                send_sem=s_send.at[k, half], recv_sem=s_recv.at[k, half],
                device_id={"ctx_1": z}, device_id_type=MESH,
            ).wait_recv()
            if half == 0:
                pltpu.make_async_remote_copy(
                    src_ref=send_d.at[0], dst_ref=recv_d.at[k], send_sem=d_send.at[k], recv_sem=d_recv.at[k],
                    device_id={"ctx_1": z}, device_id_type=MESH,
                ).wait_recv()

    def scan(half, state):
        def step(i, state):
            k = i if half == 0 else 15 - i
            s_wait(k, half)
            send_e[k, half] = state.astype(BF16)
            return recv_d[k, half : half + 1, :] * state + recv_s[k, half].astype(F32)

        state = lax.fori_loop(0, 16, step, state)
        for dy, dz in PEERS:
            e_copy(dy, dz, half).start()
        recv_e[b, half] = send_e[b, half]
        return state

    state = scan(0, jnp.zeros((64, BLK), F32))
    attend(3)
    hop(4)
    scan(1, state)
    for load in loads[9:]:
        load.wait()

    def activate(i, carry):
        rows = pl.ds(pl.multiple_of(i * 16, 16), 16)
        gate = gate_ref[0, rows, :].astype(F32)
        silu_ref[rows, :] = gate / (1.0 + jnp.exp(-gate))
        return carry

    lax.fori_loop(0, 16, activate, 0)
    attend(4)
    y_arrived(source(-way * 4))
    other_source(theirs(source(-way * 4)))

    gain = gain_ref[...]
    rows_at_once = 16

    def norm(i, carry):
        by_gain, by_skip = carry
        rows = pl.ds(pl.multiple_of(i * rows_at_once, rows_at_once), rows_at_once)
        silu = silu_ref[rows, :]
        gated = mixed[rows, :] * silu
        mean = jnp.sum(gated * gated, axis=1, keepdims=True) * (1.0 / 1024)
        inv = lax.rsqrt(mean + 1e-05)
        unit = gated * inv
        normed = unit * gain
        student_ref[0, rows, :] = normed.astype(BF16)
        grad = (normed - teacher_ref[0, rows, :].astype(F32)) * (2.0 / 8192)
        g_unit = grad * gain
        along = jnp.sum(g_unit * unit, axis=1, keepdims=True) * (1.0 / 1024)
        g_mixed = (g_unit - unit * along) * inv * silu
        a = grad * unit
        c = g_mixed * x_ref[0, rows, :].astype(F32)
        return by_gain + a[0:8] + a[8:16], by_skip + c[0:8] + c[8:16]

    zero = jnp.zeros((8, 1024), F32)
    grads = (zero, zero)
    for half in range(2):
        r0 = half * BLK
        for h in range(8):
            cols = slice(h * DH, (h + 1) * DH)
            out = acc[half, :, cols] / total[half, :, cols]
            teacher_ref[0, r0 : r0 + BLK, cols] = out.T.astype(BF16)
    outputs = (
        pltpu.make_async_copy(teacher_ref, teacher_hbm, out_sem.at[0]),
        pltpu.make_async_copy(student_ref, student_hbm, out_sem.at[1]),
    )
    outputs[0].start()
    for half in range(2):
        r0 = half * BLK
        for dy, dz in PEERS:
            e_copy(dy, dz, half, True).wait_recv()
        cmat = c_ref[0, r0 : r0 + BLK, :]
        for j in range(8):
            cols = slice(j * BLK, (j + 1) * BLK)
            flow = dot(cmat, jnp.concatenate([recv_e[j, half], recv_e[8 + j, half]], axis=0))
            mixed[r0 : r0 + BLK, cols] = mixed[r0 : r0 + BLK, cols] + flow * reach_wide[r0 : r0 + BLK, cols]
        steps = BLK // rows_at_once
        grads = lax.fori_loop(half * steps, (half + 1) * steps, norm, grads)
    by_gain = jnp.sum(grads[0], axis=0, keepdims=True)
    by_head = lax.dot_general(
        grads[1], expand, (((1,), (1,)), ((), ())), preferred_element_type=F32, precision=HIGH
    )
    by_head = jnp.sum(by_head, axis=0, keepdims=True)
    for r in range(8):
        send_g[r : r + 1, :] = by_gain[:, r * BLK : (r + 1) * BLK]
    send_g[8:9, :] = jnp.zeros((1, BLK), F32)
    send_g[8:9, 0:16] = by_head

    def g_copy(dd, dy, dz, arriving):
        where = {"dp": lax.rem(dp + dd, 2), **at(dy, dz)}
        o = where["dp"] * 16 + where["ctx_0"] * 8 + where["ctx_1"]
        slot = o if arriving else me
        return pltpu.make_async_remote_copy(
            src_ref=send_g, dst_ref=recv_g.at[slot], send_sem=g_send.at[o], recv_sem=g_recv.at[slot],
            device_id=where, device_id_type=MESH,
        )

    pl.semaphore_wait(ready, 1)
    for peer in ALL:
        g_copy(*peer, False).start()
    outputs[1].start()
    recv_g[me] = send_g[...]
    for peer in ALL:
        g_copy(*peer, True).wait_recv()
    summed = recv_g[0]
    for n in range(1, 32):
        summed = summed + recv_g[n]
    ggain_ref[...] = summed[0:8]
    gskip_ref[...] = summed[8:9, 0:16]

    for output in outputs:
        output.wait()
    for half in range(2):
        for d in range(4):
            ring(0, d, True, half).wait_send()
        for d in range(3):
            ring(0, d, False, half).wait_send()
    for zs in range(8):
        y_copy(zs, 0, True).wait_send()

        @pl.when(y == 1)
        def _():
            y_copy(zs, 1, True).wait_send()

    for dy, dz in PEERS:
        d_copy(dy, dz).wait_send()
        for half in range(2):
            s_copy(dy, dz, half).wait_send()
            e_copy(dy, dz, half).wait_send()
    for peer in ALL:
        g_copy(*peer, False).wait_send()


def hand_on(*refs):
    sources, results, held, (in_sem, out_sem) = refs[0:4], refs[4:8], refs[8:12], refs[12:]
    loads = [pltpu.make_async_copy(a, v, in_sem.at[n]) for n, (a, v) in enumerate(zip(sources, held))]
    stores = [pltpu.make_async_copy(v, a, out_sem.at[n]) for n, (v, a) in enumerate(zip(held, results))]
    for load in loads:
        load.start()
    for load, store in zip(loads, stores):
        load.wait()
        store.start()
    for store in stores:
        store.wait()


def body(
    queries, keys, values, doc_ids, inputs, gate_input, b_input, c_input, dt_raw, dt_bias, decay_log, skip, gain
):
    vmem = pl.BlockSpec(memory_space=pltpu.VMEM)
    dma = pltpu.SemaphoreType.DMA
    teacher, student, by_gain, by_skip = pl.pallas_call(
        kernel,
        out_shape=(
            jax.ShapeDtypeStruct((1, 256, 1024), BF16),
            jax.ShapeDtypeStruct((1, 256, 1024), BF16),
            jax.ShapeDtypeStruct((8, 128), F32),
            jax.ShapeDtypeStruct((1, 16), F32),
        ),
        in_specs=[pl.BlockSpec(memory_space=pl.ANY)] * 13,
        out_specs=(pl.BlockSpec(memory_space=pl.ANY),) * 2 + (vmem,) * 2,
        scratch_shapes=[
            pltpu.VMEM((1, 256, 1024), BF16),
            pltpu.VMEM((1, 256, 1024), BF16),
            pltpu.VMEM((1, 256, 1024), BF16),
            pltpu.VMEM((32, 128), jnp.int32),
            pltpu.VMEM((1, 256, 1024), BF16),
            pltpu.VMEM((1, 256, 1024), BF16),
            pltpu.VMEM((1, 256, 128), BF16),
            pltpu.VMEM((1, 256, 128), BF16),
            pltpu.VMEM((1, 16, 256), F32),
            pltpu.VMEM((1, 16), F32),
            pltpu.VMEM((1, 16), F32),
            pltpu.VMEM((1, 16), F32),
            pltpu.VMEM((1, 1024), F32),
            pltpu.VMEM((256, 1024), F32),
            pltpu.VMEM((16, 2, 2, BLK, DH), BF16),
            pltpu.VMEM((2, DH, 1024), BF16),
            pltpu.VMEM((2, DH, 1024), F32),
            pltpu.VMEM((2, 1, 1024), F32),
            pltpu.VMEM((2, 1, 1024), F32),
            pltpu.VMEM((2, 8, BLK), F32),
            pltpu.VMEM((256, 1024), F32),
            pltpu.VMEM((256, 1024), F32),
            pltpu.VMEM((16, 2, 64, BLK), BF16),
            pltpu.VMEM((16, 2, 64, BLK), BF16),
            pltpu.VMEM((8, 2, BLK), F32),
            pltpu.VMEM((16, 2, BLK), F32),
            pltpu.VMEM((16, 2, 64, BLK), BF16),
            pltpu.VMEM((16, 2, 64, BLK), BF16),
            pltpu.VMEM((9, BLK), F32),
            pltpu.VMEM((32, 9, BLK), F32),
            dma((11,)), dma((2,)), dma((2, 2)), dma((2, 4, 2)), dma((16, 2)), dma((8, 2)), dma((8, 2)),
            dma((16, 2)), dma((16, 2)), dma((16,)), dma((16,)), dma((16, 2)), dma((16, 2)), dma((32,)), dma((32,)), pltpu.SemaphoreType.REGULAR,
        ],
        compiler_params=pltpu.CompilerParams(
            collective_id=0, has_side_effects=True, vmem_limit_bytes=67043328
        ),
    )(
        queries, keys, values, doc_ids.reshape(32, 128), inputs, gate_input, b_input, c_input,
        dt_raw.transpose(0, 2, 1), dt_bias.reshape(1, 16), decay_log.reshape(1, 16), skip.reshape(1, 16),
        gain.reshape(1, 1024),
    )
    anywhere = pl.BlockSpec(memory_space=pl.ANY)
    results = (teacher, student, by_gain, by_skip)
    teacher, student, by_gain, by_skip = pl.pallas_call(
        hand_on,
        out_shape=tuple(jax.ShapeDtypeStruct(a.shape, a.dtype) for a in results),
        in_specs=[anywhere] * 4,
        out_specs=(anywhere,) * 4,
        scratch_shapes=[pltpu.VMEM(a.shape, a.dtype) for a in results] + [dma((4,)), dma((4,))],
        compiler_params=pltpu.CompilerParams(vmem_limit_bytes=67043328),
    )(*results)
    return teacher, student, by_gain.reshape(1024), by_skip.reshape(16)


def solution(mesh):
    split = Mesh(
        mesh.devices.reshape(mesh.shape["dp"], 2, 8, mesh.shape["head"]),
        ("dp", "ctx_0", "ctx_1", "head"),
    )
    rows = P("dp", CTX, "head")
    return jax.shard_map(
        body,
        mesh=split,
        in_specs=(rows, rows, rows, P("dp", None), rows, rows, rows, rows, rows)
        + (P("head"),) * 4,
        out_specs=(rows, rows, P("head"), P("head")),
        check_vma=False,
    )
```

```python
import functools

import jax
import jax.numpy as jnp
from jax import lax
from jax.experimental import pallas as pl
from jax.experimental.pallas import tpu as pltpu
from jax.sharding import Mesh
from jax.sharding import PartitionSpec as P

DH = 128
BLK = 128


def distance(dd, dy, dz):
    return min(dz, 8 - dz) + (1 if dd else 2 * dy)


PEERS = sorted(
    [(dy, dz) for dy in range(2) for dz in range(8) if (dy, dz) != (0, 0)], key=lambda p: -distance(0, *p)
)
ALL = sorted(
    [(dd, dy, dz) for dd in range(2) for dy in range(2) for dz in range(8) if (dd, dy, dz) != (0, 0, 0)],
    key=lambda p: -distance(*p),
)
MESH = pl.DeviceIdType.MESH
CTX = ("ctx_0", "ctx_1")
F32 = jnp.float32
BF16 = jnp.bfloat16
HIGH = lax.Precision.HIGHEST
LOW = -1e30
SCORE_SCALE = 1.4426950408889634 / (DH**0.5)


def iota(shape, dim):
    return lax.broadcasted_iota(jnp.int32, shape, dim)


def dot(a, b, **kw):
    return jnp.dot(a, b, preferred_element_type=F32, **kw)


def kernel(
    q_hbm, k_hbm, v_hbm, docs_hbm, x_hbm, gate_hbm, b_hbm, c_hbm, dtr_hbm, bias_hbm, decay_hbm, skip_hbm, gain_hbm,
    teacher_hbm, student_hbm, ggain_ref, gskip_ref,
    teacher_ref, student_ref, q_ref, docs_ref, x_ref, gate_ref, b_ref, c_ref, dtr_ref, bias_ref, decay_ref, skip_ref, gain_ref,
    silu_ref, kv, qt, acc, top, total, doc_start, mixed, reach_wide,
    send_s, recv_s, send_d, recv_d, send_e, recv_e, send_g, recv_g,
    in_sem, out_sem, kv_sem, ring_send, ring_recv, y_send, y_recv,
    s_send, s_recv, d_send, d_recv, e_send, e_recv, g_send, g_recv, ready,
):
    dp = lax.axis_index("dp")
    y = lax.axis_index("ctx_0")
    z = lax.axis_index("ctx_1")
    core = lax.rem(lax.axis_index("head"), 2)
    b = y * 8 + z
    me = dp * 16 + b
    way = 1 - 2 * core

    def zmod(v):
        return lax.rem(v + 16, 8)

    def at(dy, dz):
        return {"ctx_0": lax.rem(y + dy, 2), "ctx_1": zmod(z + dz)}

    barrier = pltpu.get_barrier_semaphore()
    for dy, dz in PEERS:
        pl.semaphore_signal(barrier, inc=1, device_id=at(dy, dz), device_id_type=MESH)
    partner = {"dp": 1 - dp}
    pl.semaphore_signal(barrier, inc=1, device_id=partner, device_id_type=MESH)

    arrays = (
        (docs_hbm, docs_ref), (dtr_hbm, dtr_ref), (bias_hbm, bias_ref), (decay_hbm, decay_ref),
        (skip_hbm, skip_ref), (x_hbm, x_ref), (b_hbm, b_ref), (c_hbm, c_ref),
        (q_hbm, q_ref), (gate_hbm, gate_ref), (gain_hbm, gain_ref),
    )
    loads = [pltpu.make_async_copy(src, dst, in_sem.at[n]) for n, (src, dst) in enumerate(arrays)]
    for load in loads[:8]:
        load.start()
    kv_loads = []
    for half in range(2):
        for n, src in enumerate((k_hbm, v_hbm)):
            kv_loads.append(
                pltpu.make_async_copy(
                    src.at[0, half * BLK : (half + 1) * BLK, :], kv.at[b, half, n], kv_sem.at[half, n]
                )
            )
    for load in kv_loads:
        load.start()
    for load in loads[8:]:
        load.start()
    for load in loads[:8]:
        load.wait()

    docs = docs_ref[...]
    n0 = jnp.sum(jnp.sum((docs < 1).astype(F32), axis=0, keepdims=True), axis=1, keepdims=True)
    n1 = jnp.sum(jnp.sum((docs < 2).astype(F32), axis=0, keepdims=True), axis=1, keepdims=True)

    expand = (lax.shift_right_logical(iota((16, 1024), 1), 6) == iota((16, 1024), 0)).astype(F32)

    def wide(v):
        return dot(v, expand, precision=HIGH)

    skip_wide = wide(jnp.broadcast_to(skip_ref[...], (8, 16)))[0:1]
    row_t = iota((BLK, BLK), 0)
    lane_s = iota((BLK, BLK), 1)
    row_f = row_t.astype(F32)
    lower = row_t >= lane_s
    lower_f = lower.astype(F32)
    first_lanes = lane_s < 64

    def local_terms(half):
        r0 = half * BLK
        block = b if half == 0 else 31 - b
        first = (block * BLK).astype(F32)
        doc_row = docs_ref[pl.ds(block, 1), :]
        start = jnp.where(doc_row == 0, 0.0, jnp.where(doc_row == 1, n0, n1)) - first
        end = jnp.where(doc_row == 0, n0, jnp.where(doc_row == 1, n1, 4096.0)) - first
        doc_start[half] = jnp.broadcast_to(start + first, (8, BLK))
        start_last = start[:, BLK - 1 : BLK]
        inherited = jnp.sum((start < 0.0).astype(F32), axis=1, keepdims=True)

        raw = dtr_ref[0, :, r0 : r0 + BLK].T + bias_ref[...]
        dt = jnp.maximum(raw, 0.0) + jnp.log(1.0 + jnp.exp(-jnp.abs(raw)))
        rate = -dt * jnp.exp(decay_ref[...])
        cum = dot(lower_f, rate, precision=HIGH)
        cum_t = cum.T
        dt_t = dt.T
        last = cum[BLK - 1 : BLK, :]
        rows16 = iota((BLK, 16), 0).astype(F32)
        tail = jnp.where(rows16 >= start_last, jnp.exp(last - cum) * dt, 0.0)
        reach = jnp.where(rows16 < inherited, jnp.exp(cum), 0.0)
        decay = jnp.where(start_last < 0.0, jnp.exp(last), 0.0)
        tail_wide = wide(tail)
        decay_wide = wide(jnp.broadcast_to(decay, (8, 16)))[0:1]

        bmat = b_ref[0, r0 : r0 + BLK, :]
        cmat = c_ref[0, r0 : r0 + BLK, :]
        loaded = (x_ref[0, r0 : r0 + BLK, :].astype(F32) * tail_wide).astype(BF16)
        state = dot(bmat.T, loaded).astype(BF16)
        for j in range(8):
            cols = slice(j * BLK, (j + 1) * BLK)
            send_d[j, half : half + 1, :] = decay_wide[:, cols]
            for n in range(2):
                send_s[n * 8 + j, half] = state[n * 64 : n * 64 + 64, cols]

        def rest():
            reach_wide[r0 : r0 + BLK, :] = wide(reach)
            gram = lax.dot_general(cmat, bmat, (((1,), (1,)), ((), ())), preferred_element_type=F32)
            gram = jnp.where(lower & (row_f < end), gram, 0.0)
            for j in range(8):
                cols = slice(j * BLK, (j + 1) * BLK)
                pair = x_ref[0, r0 : r0 + BLK, cols]
                parts = []
                for h in (2 * j, 2 * j + 1):
                    fading = jnp.exp(cum[:, h : h + 1] - cum_t[h : h + 1, :])
                    parts.append((fading * (gram * dt_t[h : h + 1, :])).astype(BF16))
                zero = jnp.zeros_like(pair)
                stacked = jnp.concatenate(
                    [jnp.where(first_lanes, pair, zero), jnp.where(first_lanes, zero, pair)], axis=0
                )
                intra = dot(jnp.concatenate(parts, axis=1), stacked)
                mixed[r0 : r0 + BLK, cols] = intra + skip_wide[:, cols] * pair.astype(F32)

        return rest

    def source(off):
        return zmod(z + off)

    def ring(off, dist, forward, half):
        s = y * 8 + source(off)
        lane = 0 if forward else 1
        return pltpu.make_async_remote_copy(
            src_ref=kv.at[s, half], dst_ref=kv.at[s, half],
            send_sem=ring_send.at[lane, dist, half], recv_sem=ring_recv.at[s, half],
            device_id={"ctx_1": zmod(z + (way if forward else -way))}, device_id_type=MESH,
        )

    def wanted(zs, forward, gone):
        sign = way if forward else -way
        some = y == 1
        for k in range(gone + 1, 5 if forward else 4):
            some = some | (zmod(zs + sign * k) < zs)
        return some

    def ring_start(off, dist, forward, half):
        if half == 0:
            ring(off, dist, forward, 0).start()
        else:

            @pl.when(wanted(source(off), forward, dist))
            def _():
                ring(off, dist, forward, 1).start()

    def ring_arrived(off, dist, forward, half):
        if half == 0:
            ring(off, 0, forward, 0).wait_recv()
        else:

            @pl.when(wanted(source(off), forward, dist - 1))
            def _():
                ring(off, 0, forward, 1).wait_recv()

    def y_copy(zs, half, mine):
        s = (y if mine else 1 - y) * 8 + zs
        return pltpu.make_async_remote_copy(
            src_ref=kv.at[s, half], dst_ref=kv.at[s, half],
            send_sem=y_send.at[zs, half], recv_sem=y_recv.at[zs, half],
            device_id={"ctx_0": 1 - y}, device_id_type=MESH,
        )

    def y_start(zs, half):
        if half == 0:
            y_copy(zs, 0, True).start()
        else:

            @pl.when(y == 1)
            def _():
                y_copy(zs, 1, True).start()

    def y_arrived(zs):
        y_copy(zs, 0, False).wait_recv()

        @pl.when(y == 0)
        def _():
            y_copy(zs, 1, False).wait_recv()

    def owner(dy, dz):
        other = at(dy, dz)
        return other, other["ctx_0"] * 8 + other["ctx_1"]

    def s_copy(dy, dz, half):
        other, o = owner(dy, dz)
        return pltpu.make_async_remote_copy(
            src_ref=send_s.at[o, half], dst_ref=recv_s.at[b, half],
            send_sem=s_send.at[o, half], recv_sem=s_recv.at[b, half],
            device_id=other, device_id_type=MESH,
        )

    def d_copy(dy, dz):
        other, o = owner(dy, dz)
        return pltpu.make_async_remote_copy(
            src_ref=send_d.at[other["ctx_1"]], dst_ref=recv_d.at[b], send_sem=d_send.at[o], recv_sem=d_recv.at[b],
            device_id=other, device_id_type=MESH,
        )

    def e_copy(dy, dz, half, arriving=False):
        other, o = owner(dy, dz)
        slot = o if arriving else b
        return pltpu.make_async_remote_copy(
            src_ref=send_e.at[o, half], dst_ref=recv_e.at[slot, half],
            send_sem=e_send.at[o, half], recv_sem=e_recv.at[slot, half],
            device_id=other, device_id_type=MESH,
        )

    rests = [local_terms(0)]
    for load in kv_loads:
        load.wait()
    pl.semaphore_wait(barrier, len(PEERS) + 1)
    pl.semaphore_signal(ready, inc=1, device_id=partner, device_id_type=MESH)
    for half in range(2):
        ring_start(0, 0, True, half)
        ring_start(0, 0, False, half)
        y_start(z, half)
    for dy, dz in PEERS[:8]:
        s_copy(dy, dz, 0).start()
    rests.append(local_terms(1))
    for rest in rests:
        rest()

    loads[8].wait()
    for half in range(2):
        for h in range(8):
            qt[half, :, h * DH : (h + 1) * DH] = q_ref[
                0, half * BLK : (half + 1) * BLK, h * DH : (h + 1) * DH
            ].T
    top[...] = jnp.full(top.shape, LOW, F32)
    total[...] = jnp.zeros(total.shape, F32)
    acc[...] = jnp.zeros(acc.shape, F32)

    def item(s, kh, qh, diagonal):
        key = kv[s, kh, 0]
        value_t = kv[s, kh, 1].T
        key_block = jnp.where(kh == 0, s, 31 - s) if not isinstance(kh, int) else (s if kh == 0 else 31 - s)
        start = doc_start[qh][0:1] - (key_block * BLK).astype(F32)
        allowed = row_f >= start
        if diagonal:
            allowed = allowed & (row_t <= lane_s)
        bias = jnp.where(allowed, 0.0, LOW)
        bias = jnp.concatenate([bias, bias], axis=1)
        for c in range(4):
            cols = slice(c * 256, (c + 1) * 256)
            scores = dot(key, qt[qh, :, cols]) * SCORE_SCALE + bias
            old = top[qh, :, cols]
            new = jnp.maximum(old, jnp.max(scores, axis=0, keepdims=True))
            weights = jnp.exp2(scores - new)
            factor = jnp.exp2(old - new)
            total[qh, :, cols] = total[qh, :, cols] * factor + jnp.sum(weights, axis=0, keepdims=True)
            acc[qh, :, cols] = acc[qh, :, cols] * factor + dot(value_t, weights.astype(BF16))
            top[qh, :, cols] = new

    def other_source(s):
        item(s, 0, 1, False)
        pick = jnp.where(s < b, 0, 1)
        item(s, pick, pick, False)

    def sources(ids):
        def step(i, carry):
            s = ids[0]
            for n in range(1, len(ids)):
                s = jnp.where(i == n, ids[n], s)
            other_source(s)
            return carry

        lax.fori_loop(0, len(ids), step, 0)

    def mine(zs):
        return y * 8 + zs

    def theirs(zs):
        return (1 - y) * 8 + zs

    def hop(d):
        up = source(-way * d)
        down = source(way * d)
        for half in range(2):
            ring_arrived(-way * d, d, True, half)
            if d < 4:
                ring_start(-way * d, d, True, half)
            y_start(up, half)
            if d < 4:
                ring_arrived(way * d, d, False, half)
                if d < 3:
                    ring_start(way * d, d, False, half)
                y_start(down, half)

    def attend(d):
        ids = [mine(source(-way * d))]
        if d < 4:
            ids.append(mine(source(way * d)))
        if d == 1:
            y_arrived(z)
            ids.append(theirs(z))
        else:
            for off in (-way * (d - 1), way * (d - 1)):
                y_arrived(source(off))
                ids.append(theirs(source(off)))
        sources(ids)

    item(b, 0, 0, True)
    item(b, 1, 1, True)
    item(b, 0, 1, False)

    hop(1)
    recv_s[b] = send_s[b]
    recv_d[b] = send_d[z]
    for dy, dz in PEERS:
        d_copy(dy, dz).start()
    for dy, dz in PEERS[8:]:
        s_copy(dy, dz, 0).start()
    hop(2)
    for dy, dz in PEERS:
        s_copy(dy, dz, 1).start()
    attend(1)
    hop(3)
    attend(2)

    def s_wait(k, half):
        @pl.when(k != b)
        def _():
            pltpu.make_async_remote_copy(
                src_ref=send_s.at[k, half], dst_ref=recv_s.at[k, half],
                send_sem=s_send.at[k, half], recv_sem=s_recv.at[k, half],
                device_id={"ctx_1": z}, device_id_type=MESH,
            ).wait_recv()
            if half == 0:
                pltpu.make_async_remote_copy(
                    src_ref=send_d.at[0], dst_ref=recv_d.at[k], send_sem=d_send.at[k], recv_sem=d_recv.at[k],
                    device_id={"ctx_1": z}, device_id_type=MESH,
                ).wait_recv()

    def scan(half, state):
        def step(i, state):
            k = i if half == 0 else 15 - i
            s_wait(k, half)
            send_e[k, half] = state.astype(BF16)
            return recv_d[k, half : half + 1, :] * state + recv_s[k, half].astype(F32)

        state = lax.fori_loop(0, 16, step, state)
        for dy, dz in PEERS:
            e_copy(dy, dz, half).start()
        recv_e[b, half] = send_e[b, half]
        return state

    state = scan(0, jnp.zeros((64, BLK), F32))
    attend(3)
    hop(4)
    scan(1, state)
    for load in loads[9:]:
        load.wait()

    def activate(i, carry):
        rows = pl.ds(pl.multiple_of(i * 16, 16), 16)
        gate = gate_ref[0, rows, :].astype(F32)
        silu_ref[rows, :] = gate / (1.0 + jnp.exp(-gate))
        return carry

    lax.fori_loop(0, 16, activate, 0)
    attend(4)
    y_arrived(source(-way * 4))
    other_source(theirs(source(-way * 4)))

    gain = gain_ref[...]
    rows_at_once = 16

    def norm(i, carry):
        by_gain, by_skip = carry
        rows = pl.ds(pl.multiple_of(i * rows_at_once, rows_at_once), rows_at_once)
        silu = silu_ref[rows, :]
        gated = mixed[rows, :] * silu
        mean = jnp.sum(gated * gated, axis=1, keepdims=True) * (1.0 / 1024)
        inv = lax.rsqrt(mean + 1e-05)
        unit = gated * inv
        normed = unit * gain
        student_ref[0, rows, :] = normed.astype(BF16)
        grad = (normed - teacher_ref[0, rows, :].astype(F32)) * (2.0 / 8192)
        g_unit = grad * gain
        along = jnp.sum(g_unit * unit, axis=1, keepdims=True) * (1.0 / 1024)
        g_mixed = (g_unit - unit * along) * inv * silu
        a = grad * unit
        c = g_mixed * x_ref[0, rows, :].astype(F32)
        return by_gain + a[0:8] + a[8:16], by_skip + c[0:8] + c[8:16]

    zero = jnp.zeros((8, 1024), F32)
    grads = (zero, zero)
    for half in range(2):
        r0 = half * BLK
        for h in range(8):
            cols = slice(h * DH, (h + 1) * DH)
            out = acc[half, :, cols] / total[half, :, cols]
            teacher_ref[0, r0 : r0 + BLK, cols] = out.T.astype(BF16)
    outputs = (
        pltpu.make_async_copy(teacher_ref, teacher_hbm, out_sem.at[0]),
        pltpu.make_async_copy(student_ref, student_hbm, out_sem.at[1]),
    )
    outputs[0].start()
    for half in range(2):
        r0 = half * BLK
        for dy, dz in PEERS:
            e_copy(dy, dz, half, True).wait_recv()
        cmat = c_ref[0, r0 : r0 + BLK, :]
        for j in range(8):
            cols = slice(j * BLK, (j + 1) * BLK)
            flow = dot(cmat, jnp.concatenate([recv_e[j, half], recv_e[8 + j, half]], axis=0))
            mixed[r0 : r0 + BLK, cols] = mixed[r0 : r0 + BLK, cols] + flow * reach_wide[r0 : r0 + BLK, cols]
        steps = BLK // rows_at_once
        grads = lax.fori_loop(half * steps, (half + 1) * steps, norm, grads)
    by_gain = jnp.sum(grads[0], axis=0, keepdims=True)
    by_head = lax.dot_general(
        grads[1], expand, (((1,), (1,)), ((), ())), preferred_element_type=F32, precision=HIGH
    )
    by_head = jnp.sum(by_head, axis=0, keepdims=True)
    for r in range(8):
        send_g[r : r + 1, :] = by_gain[:, r * BLK : (r + 1) * BLK]
    send_g[8:9, :] = jnp.zeros((1, BLK), F32)
    send_g[8:9, 0:16] = by_head

    def g_copy(dd, dy, dz, arriving):
        where = {"dp": lax.rem(dp + dd, 2), **at(dy, dz)}
        o = where["dp"] * 16 + where["ctx_0"] * 8 + where["ctx_1"]
        slot = o if arriving else me
        return pltpu.make_async_remote_copy(
            src_ref=send_g, dst_ref=recv_g.at[slot], send_sem=g_send.at[o], recv_sem=g_recv.at[slot],
            device_id=where, device_id_type=MESH,
        )

    pl.semaphore_wait(ready, 1)
    for peer in ALL:
        g_copy(*peer, False).start()
    outputs[1].start()
    recv_g[me] = send_g[...]
    for peer in ALL:
        g_copy(*peer, True).wait_recv()
    summed = recv_g[0]
    for n in range(1, 32):
        summed = summed + recv_g[n]
    ggain_ref[...] = summed[0:8]
    gskip_ref[...] = summed[8:9, 0:16]

    for output in outputs:
        output.wait()
    for d in range(4):
        ring(0, d, True, 0).wait_send()

        @pl.when(wanted(source(-way * d), True, d))
        def _():
            ring(0, d, True, 1).wait_send()

    for d in range(3):
        ring(0, d, False, 0).wait_send()

        @pl.when(wanted(source(way * d), False, d))
        def _():
            ring(0, d, False, 1).wait_send()

    for zs in range(8):
        y_copy(zs, 0, True).wait_send()

        @pl.when(y == 1)
        def _():
            y_copy(zs, 1, True).wait_send()

    for dy, dz in PEERS:
        d_copy(dy, dz).wait_send()
        for half in range(2):
            s_copy(dy, dz, half).wait_send()
            e_copy(dy, dz, half).wait_send()
    for peer in ALL:
        g_copy(*peer, False).wait_send()


def hand_on(*refs):
    sources, results, held, (in_sem, out_sem) = refs[0:4], refs[4:8], refs[8:12], refs[12:]
    loads = [pltpu.make_async_copy(a, v, in_sem.at[n]) for n, (a, v) in enumerate(zip(sources, held))]
    stores = [pltpu.make_async_copy(v, a, out_sem.at[n]) for n, (v, a) in enumerate(zip(held, results))]
    for load in loads:
        load.start()
    for load, store in zip(loads, stores):
        load.wait()
        store.start()
    for store in stores:
        store.wait()


def body(
    queries, keys, values, doc_ids, inputs, gate_input, b_input, c_input, dt_raw, dt_bias, decay_log, skip, gain
):
    vmem = pl.BlockSpec(memory_space=pltpu.VMEM)
    dma = pltpu.SemaphoreType.DMA
    teacher, student, by_gain, by_skip = pl.pallas_call(
        kernel,
        out_shape=(
            jax.ShapeDtypeStruct((1, 256, 1024), BF16),
            jax.ShapeDtypeStruct((1, 256, 1024), BF16),
            jax.ShapeDtypeStruct((8, 128), F32),
            jax.ShapeDtypeStruct((1, 16), F32),
        ),
        in_specs=[pl.BlockSpec(memory_space=pl.ANY)] * 13,
        out_specs=(pl.BlockSpec(memory_space=pl.ANY),) * 2 + (vmem,) * 2,
        scratch_shapes=[
            pltpu.VMEM((1, 256, 1024), BF16),
            pltpu.VMEM((1, 256, 1024), BF16),
            pltpu.VMEM((1, 256, 1024), BF16),
            pltpu.VMEM((32, 128), jnp.int32),
            pltpu.VMEM((1, 256, 1024), BF16),
            pltpu.VMEM((1, 256, 1024), BF16),
            pltpu.VMEM((1, 256, 128), BF16),
            pltpu.VMEM((1, 256, 128), BF16),
            pltpu.VMEM((1, 16, 256), F32),
            pltpu.VMEM((1, 16), F32),
            pltpu.VMEM((1, 16), F32),
            pltpu.VMEM((1, 16), F32),
            pltpu.VMEM((1, 1024), F32),
            pltpu.VMEM((256, 1024), F32),
            pltpu.VMEM((16, 2, 2, BLK, DH), BF16),
            pltpu.VMEM((2, DH, 1024), BF16),
            pltpu.VMEM((2, DH, 1024), F32),
            pltpu.VMEM((2, 1, 1024), F32),
            pltpu.VMEM((2, 1, 1024), F32),
            pltpu.VMEM((2, 8, BLK), F32),
            pltpu.VMEM((256, 1024), F32),
            pltpu.VMEM((256, 1024), F32),
            pltpu.VMEM((16, 2, 64, BLK), BF16),
            pltpu.VMEM((16, 2, 64, BLK), BF16),
            pltpu.VMEM((8, 2, BLK), F32),
            pltpu.VMEM((16, 2, BLK), F32),
            pltpu.VMEM((16, 2, 64, BLK), BF16),
            pltpu.VMEM((16, 2, 64, BLK), BF16),
            pltpu.VMEM((9, BLK), F32),
            pltpu.VMEM((32, 9, BLK), F32),
            dma((11,)), dma((2,)), dma((2, 2)), dma((2, 4, 2)), dma((16, 2)), dma((8, 2)), dma((8, 2)),
            dma((16, 2)), dma((16, 2)), dma((16,)), dma((16,)), dma((16, 2)), dma((16, 2)), dma((32,)), dma((32,)), pltpu.SemaphoreType.REGULAR,
        ],
        compiler_params=pltpu.CompilerParams(
            collective_id=0, has_side_effects=True, vmem_limit_bytes=67043328
        ),
    )(
        queries, keys, values, doc_ids.reshape(32, 128), inputs, gate_input, b_input, c_input,
        dt_raw.transpose(0, 2, 1), dt_bias.reshape(1, 16), decay_log.reshape(1, 16), skip.reshape(1, 16),
        gain.reshape(1, 1024),
    )
    anywhere = pl.BlockSpec(memory_space=pl.ANY)
    results = (teacher, student, by_gain, by_skip)
    teacher, student, by_gain, by_skip = pl.pallas_call(
        hand_on,
        out_shape=tuple(jax.ShapeDtypeStruct(a.shape, a.dtype) for a in results),
        in_specs=[anywhere] * 4,
        out_specs=(anywhere,) * 4,
        scratch_shapes=[pltpu.VMEM(a.shape, a.dtype) for a in results] + [dma((4,)), dma((4,))],
        compiler_params=pltpu.CompilerParams(vmem_limit_bytes=67043328),
    )(*results)
    return teacher, student, by_gain.reshape(1024), by_skip.reshape(16)


def solution(mesh):
    split = Mesh(
        mesh.devices.reshape(mesh.shape["dp"], 2, 8, mesh.shape["head"]),
        ("dp", "ctx_0", "ctx_1", "head"),
    )
    rows = P("dp", CTX, "head")
    return jax.shard_map(
        body,
        mesh=split,
        in_specs=(rows, rows, rows, P("dp", None), rows, rows, rows, rows, rows)
        + (P("head"),) * 4,
        out_specs=(rows, rows, P("head"), P("head")),
        check_vma=False,
    )
```
